512 devices in a mesh: band: 8 (over x, core), blk: 64 (over y, z).
Axes of the slice: x: 4, y: 4, z: 16, core: 2. Of those that a mesh axis runs over, the one named last changes fastest.
Arguments:
- amps: bfloat16 [2560, 64, 128], P(None, 'blk'), may hold values from -6 to 6
- beam: float32 [8, 2560], P('band'), may hold values from 0.2 to 1
- legendre: bfloat16 [64, 2560, 256], P('blk'), as said below
- m_values: int32 [64], replicated, may hold values from 0 to 2559, as said below
- cycle_order: int32 [256], replicated, may hold values from 0 to 255, each once
- pixel_counts: int32 [256], replicated, may hold values from 512 to 4096, as said below
- inv_noise: float32 [8, 256, 4096], P('band', 'blk'), may hold values from 0.1 to 2
Outputs:
- amps_out: float32 [2560, 64, 128], P('band', 'blk')
The draws below stay inside these ranges and needn't reach their ends.
Inputs may be any that keep to these rules, and one draw needn't show every extreme that they name: `m_values`: distinct orders; both 0 and 2559 occur. legendre[m, l, s] is zero wherever l < m_values[m]. `pixel_counts`: some cycle has exactly 4096 pixels.
All inputs are finite; a program needn't handle non-finite values.
Results may differ from the reference program's by a relative error of at most 0.0017.
Values may be sent and summed in bfloat16 or wider, within the bound.
A program may use at most 64 MiB of HBM per device.

```python
import math
import jax
import jax.numpy as jnp
from jax import lax

DEGREES = 2560
PIX = 4096
CHAINS = 64
BANDS = 8
ORDERS = 64
CYCLES = 256


def drawn_orders(key):
    base_key = jax.random.fold_in(key, 11)
    inner = 1 + jax.random.permutation(jax.random.fold_in(base_key, 1), DEGREES - 2)[:ORDERS - 2]
    chosen = jnp.concatenate([jnp.array([0, DEGREES - 1], jnp.int32), inner.astype(jnp.int32)])
    return jax.random.permutation(jax.random.fold_in(base_key, 2), chosen).astype(jnp.int32)


def draw_m_values(key, part):
    return drawn_orders(key)


def draw_legendre(key, part):
    orders_now = drawn_orders(key)
    values = jax.random.normal(jax.random.fold_in(key, 12), (ORDERS, DEGREES, CYCLES), jnp.float32)
    values = values * jnp.float32((DEGREES * CYCLES) ** (-0.25))
    degree_idx = jnp.arange(DEGREES, dtype=jnp.int32)
    keep = degree_idx[None, :, None] >= orders_now[:, None, None]
    return jnp.where(keep, values, jnp.float32(0.0)).astype(jnp.bfloat16)


def draw_pixel_counts(key, part):
    counts_drawn = jax.random.randint(jax.random.fold_in(key, 13), (CYCLES,), PIX // 8, PIX + 1).astype(jnp.int32)
    position = jax.random.randint(jax.random.fold_in(key, 14), (), 0, CYCLES)
    return counts_drawn.at[position].set(PIX).astype(jnp.int32)


def shard_levels(stream_key, shape, pieces, smallest, high):
    level = 1.0
    for dim, blocks in pieces:
        steps = jax.random.uniform(jax.random.fold_in(jax.random.fold_in(stream_key, 6), dim), (blocks,), jnp.float32, smallest / len(pieces), high / len(pieces))
        level = level * jnp.repeat(jnp.exp(steps), shape[dim] // blocks).reshape((-1,) + (1,) * (len(shape) - 1 - dim))
    return level


def bell_draw(own_key, shape, spread, most, cuts=(), held_as=jnp.bfloat16):
    loudness = shard_levels(own_key, shape, cuts, -0.22, 0.18) if cuts else 1.0
    entries = jax.random.normal(own_key, shape, jnp.float32) * spread * loudness
    return jnp.minimum(jnp.maximum(entries, -most), most).astype(held_as)


def setup_inputs(seed: int = 0) -> dict:
    key_list = jax.random.split(jax.random.key(seed), 8)
    return {
        "amps": bell_draw(key_list[0], (DEGREES, ORDERS, 2 * CHAINS), 1.0, 6.0, ((1, 64),)),
        "beam": jnp.clip(jnp.exp(math.log(1.0) - 1.609438 * jax.random.uniform(key_list[1], (BANDS, DEGREES), jnp.float32) ** shard_levels(key_list[1], (BANDS, DEGREES), ((0, 8),), -0.2, 0.2)), 0.2, 1.0),
        "legendre": draw_legendre(jax.random.fold_in(key_list[7], 71), 0),
        "m_values": draw_m_values(jax.random.fold_in(key_list[7], 71), 0),
        "cycle_order": jax.random.permutation(key_list[4], CYCLES).astype(jnp.int32),
        "pixel_counts": draw_pixel_counts(jax.random.fold_in(key_list[7], 71), 0),
        "inv_noise": jnp.clip(jnp.exp(math.log(2.0) - 2.9957323 * jax.random.uniform(key_list[6], (BANDS, CYCLES, PIX), jnp.float32) ** shard_levels(key_list[6], (BANDS, CYCLES, PIX), ((0, 8), (1, 64)), -0.2, 0.2)), 0.1, 2.0),
    }


def cycle_table(order_ids, cycle_id, pixel_count, pixels):
    pixel_idx = jnp.arange(pixels, dtype=jnp.int32)
    product_mod = order_ids[:, None] * pixel_idx[None, :] % pixel_count
    parity = cycle_id % 2
    numerator = (2 * product_mod + order_ids[:, None] * parity) % (2 * pixel_count)
    phase_angle = numerator.astype(jnp.float32) * (jnp.float32(math.pi) / pixel_count.astype(jnp.float32))
    inside = (pixel_idx < pixel_count)[None, :]
    norm_scale = lax.rsqrt(pixel_count.astype(jnp.float32))
    cos_part = jnp.where(inside, jnp.cos(phase_angle) * norm_scale, jnp.float32(0.0))
    sin_part = jnp.where(inside, -jnp.sin(phase_angle) * norm_scale, jnp.float32(0.0))
    return jnp.stack([cos_part, sin_part], axis=1).reshape(2 * order_ids.shape[0], pixels)

def cycle_pass(modes_in, phase_table, weights):
    orders = modes_in.shape[0]
    chains = modes_in.shape[1] // 2
    modes_flat = modes_in.reshape(2 * orders, chains)
    pixel_field = lax.dot_general(modes_flat, phase_table, (((0,), (0,)), ((), ())), precision=lax.Precision.HIGHEST)
    weighted_field = pixel_field * weights[None, :]
    projected = lax.dot_general(phase_table, weighted_field, (((1,), (1,)), ((), ())), precision=lax.Precision.HIGHEST)
    return projected.reshape(orders, 2 * chains)

def reference(amps, beam, legendre, m_values, cycle_order, pixel_counts, inv_noise):
    accum = jnp.zeros(amps.shape, jnp.float32)
    amps_major = jnp.swapaxes(amps, 0, 1)
    for band_idx in range(BANDS):
        gains = beam[band_idx]
        weighted = (amps_major.astype(jnp.float32) * gains[None, :, None]).astype(jnp.bfloat16)

        def synth_one(packed):
            return lax.dot_general(packed[0], packed[1], (((0,), (0,)), ((), ())), preferred_element_type=jnp.float32)
        synth = lax.map(synth_one, (legendre, weighted))
        cycle_major = jnp.swapaxes(synth, 0, 1)
        cycle_counts = pixel_counts[cycle_order]

        def cycle_one(packed):
            phase_table = cycle_table(m_values, packed[1], packed[2], PIX)
            return cycle_pass(packed[0], phase_table, packed[3])
        projected = lax.map(cycle_one, (cycle_major, cycle_order, cycle_counts, inv_noise[band_idx]))
        proj_half = jnp.swapaxes(projected.astype(jnp.bfloat16), 0, 1)

        def analyse_one(packed):
            return jnp.dot(packed[0], packed[1], preferred_element_type=jnp.float32)
        analysed = lax.map(analyse_one, (legendre, proj_half))
        accum = accum + jnp.swapaxes(analysed, 0, 1) * gains[:, None, None]
    return accum
```

```python
import functools
import math

import jax
import jax.numpy as jnp
from jax import lax
from jax.experimental import pallas as pl
from jax.experimental.pallas import tpu as pltpu
from jax.sharding import PartitionSpec as P

MESH = pl.DeviceIdType.MESH
F32, BF16, I32 = jnp.float32, jnp.bfloat16, jnp.int32
LANES = 128
WIDE = 512
NY = 4


def dot_nt(a, b):
    return lax.dot_general(a, b, (((1,), (1,)), ((), ())), preferred_element_type=F32)


def split(x):
    high = x.astype(BF16)
    return high, (x - high.astype(F32)).astype(BF16)


def remainder(x, count, inverse):
    r = x - jnp.floor(x * inverse) * count
    r = jnp.where(r < 0.0, r + count, r)
    return jnp.where(r >= count, r - count, r)


def turn(doubled, count, inverse):
    k = jnp.floor(doubled * inverse + 0.5)
    phi = (doubled - k * count) * (inverse * jnp.float32(math.pi / 2))
    sq = phi * phi
    sin = phi + phi * sq * (-1.6666654611e-1 + sq * (8.3321608736e-3 + sq * -1.9515295891e-4))
    cos = 1.0 - 0.5 * sq + sq * sq * (
        4.166664568298827e-2 + sq * (-1.388731625493765e-3 + sq * 2.443315711809948e-5)
    )
    ki = k.astype(I32)
    odd = (ki & 1) == 1
    c = jnp.where(odd, sin, cos)
    s = jnp.where(odd, cos, sin)
    return jnp.where(((ki + 1) & 2) != 0, -c, c), jnp.where((ki & 2) != 0, s, -s)


def kernel(
    nband, nblk,
    m_ref, order_ref, counts_ref, amps_ref, beam_ref, leg_ref, noise_ref,
    out_ref,
    m_col, a_cos, a_sin, b_cos, b_sin, gram, flat, syn, got, stage, half, back, around, legp, beams, gains, inside,
    send_sem, recv_sem, own_sem, beam_sem, ag_send, ag_recv, fw_send, fw_recv,
):
    band = lax.axis_index("band")
    me = lax.axis_index("blk")
    nz = nblk // NY
    nx = nband // 2
    degrees = leg_ref.shape[0]
    cycles = leg_ref.shape[1]
    orders = m_col.shape[0]
    here = cycles // nblk
    pixels = noise_ref.shape[1]
    steps = pixels // WIDE
    chains = amps_ref.shape[1] // 2
    rows = degrees // nband
    my_y, my_z = me // nz, me % nz
    my_x, core = band // 2, band % 2

    def other_blk(t):
        u, v = t // NY, t % NY
        dz = nz // 2 + jnp.where(u % 2 == 0, u // 2, -((u + 1) // 2))
        return (my_y + v + 1) % NY * nz + (my_z + dz + nz) % nz

    def band_of(dx, dc):
        return (my_x + dx + nx) % nx * 2 + (core + dc) % 2

    others = [(dx, dc) for dx in range(nx) for dc in range(2) if (dx, dc) != (0, 0)]

    barrier = pltpu.get_barrier_semaphore()

    @pl.loop(0, nblk - 1)
    def _(t):
        pl.semaphore_signal(barrier, inc=1, device_id=(band, other_blk(t)), device_id_type=MESH)

    for dx, dc in others:
        pl.semaphore_signal(barrier, inc=1, device_id=(band_of(dx, dc), me), device_id_type=MESH)

    def synth_step(i, total):
        parts = []
        for h in range(2):
            at = pl.multiple_of(i * 2 * LANES + h * LANES, LANES)
            piece = amps_ref[pl.ds(at, LANES), :].astype(F32).T
            parts.append((piece * beam_ref[:, pl.ds(at, LANES)]).astype(BF16))
        weighted = jnp.concatenate(parts, axis=1)
        at = pl.multiple_of(i * 2 * LANES, LANES)
        return total + jnp.dot(weighted, leg_ref[pl.ds(at, 2 * LANES), :], preferred_element_type=F32)

    total = lax.fori_loop(0, degrees // (2 * LANES), synth_step, jnp.zeros((2 * chains, cycles), F32))
    flat[...] = total.T
    for i in range(here):
        syn[:, i, :] = flat[pl.ds(i, nblk, stride=here), :]

    @pl.loop(0, orders)
    def _(i):
        m_col[pl.ds(i, 1), :] = jnp.full((1, LANES), m_ref[i], I32).astype(F32)

    lane = lax.broadcasted_iota(I32, (1, LANES), 1)

    def cycle(i):
        q = order_ref[me * here + i]
        return counts_ref[q], q & 1

    m = m_col[...]
    count_v = jnp.full((1, LANES), 1, I32)
    parity_v = jnp.zeros((1, LANES), I32)
    pixel = lax.broadcasted_iota(I32, (1, pixels), 1)
    for i in range(here):
        n, parity = cycle(i)
        inside[i] = jnp.where(pixel < n, noise_ref[i : i + 1, :], 0.0)
        mine = lane // steps == i
        count_v = jnp.where(mine, n, count_v)
        parity_v = jnp.where(mine, parity, parity_v)
    count_v = count_v.astype(F32)
    inverse_v = 1.0 / count_v
    r = remainder(m * ((lane % steps) * WIDE).astype(F32), count_v, inverse_v)
    ca, sa = turn(4.0 * r + 2.0 * m * parity_v.astype(F32), count_v, inverse_v)
    for t in range(here * steps):
        a_cos[t] = jnp.broadcast_to(ca[:, t : t + 1], (orders, LANES))
        a_sin[t] = jnp.broadcast_to(sa[:, t : t + 1], (orders, LANES))

    def form_gram(i):
        n, _ = cycle(i)
        count = jnp.full((1, LANES), n, I32).astype(F32)
        inverse = 1.0 / count
        for g in range(WIDE // LANES):
            r = remainder(m_col[...] * (lane + g * LANES).astype(F32), count, inverse)
            c, s = turn(4.0 * r, count, inverse)
            b_cos[:, g * LANES : (g + 1) * LANES] = c
            b_sin[:, g * LANES : (g + 1) * LANES] = s

        def step(a, acc):
            c1, s1 = a_cos[i * steps + a], a_sin[i * steps + a]
            left, right = [], []
            for g in range(WIDE // LANES):
                c2, s2 = b_cos[:, g * LANES : (g + 1) * LANES], b_sin[:, g * LANES : (g + 1) * LANES]
                at = pl.multiple_of(a * WIDE + g * LANES, LANES)
                w = inside[i, :, pl.ds(at, LANES)]
                c = c1 * c2 - s1 * s2
                s = s1 * c2 + c1 * s2
                ch, cl = split(c)
                sh, sl = split(s)
                left.append(jnp.concatenate([ch, sh, cl, sl], axis=0))
                ch, cl = split(c * w)
                sh, sl = split(s * w)
                right.append(jnp.concatenate([ch, sh, cl, sl], axis=0))
            return acc + dot_nt(jnp.concatenate(left, axis=1), jnp.concatenate(right, axis=1))

        acc = lax.fori_loop(0, steps, step, jnp.zeros((4 * orders, 4 * orders), F32))
        two = 2 * orders
        full = (acc[:two, :two] + acc[:two, two:]) + (acc[two:, :two] + acc[two:, two:])
        full = full * inverse[:, :two] if two <= LANES else full * inverse[:, :1]
        full = jnp.concatenate([full[:orders], pltpu.roll(full[orders:], orders, 1)], axis=0)
        gram[i] = jnp.concatenate(split(full), axis=0)

    @pl.loop(0, here // 2)
    def _(i):
        form_gram(i)

    pl.semaphore_wait(barrier, nblk - 1 + nband - 1)

    @pl.loop(0, nblk - 1)
    def _(t):
        d = other_blk(t)
        pltpu.make_async_remote_copy(
            src_ref=syn.at[d], dst_ref=got.at[me], send_sem=send_sem.at[0], recv_sem=recv_sem.at[0],
            device_id=(band, d), device_id_type=MESH,
        ).start()

    pltpu.make_async_copy(syn.at[me], got.at[me], own_sem.at[0]).start()
    for dx, dc in others:
        pltpu.make_async_remote_copy(
            src_ref=beam_ref, dst_ref=beams.at[band], send_sem=beam_sem.at[0], recv_sem=beam_sem.at[1],
            device_id=(band_of(dx, dc), me), device_id_type=MESH,
        ).start()
    pltpu.make_async_copy(beam_ref, beams.at[band], own_sem.at[1]).start()

    @pl.loop(here // 2, here)
    def _(i):
        form_gram(i)

    row = lax.broadcasted_iota(I32, (cycles, cycles), 0)
    col = lax.broadcasted_iota(I32, (cycles, cycles), 1)
    pick = jnp.where(row == here * (col % nblk) + col // nblk, 1.0, 0.0).astype(BF16)
    mine = leg_ref[pl.ds(pl.multiple_of(band * rows, rows & -rows), rows), :]
    legp[...] = jnp.dot(mine, pick, preferred_element_type=F32).astype(BF16)

    pltpu.make_async_copy(syn.at[me], got.at[me], own_sem.at[0]).wait()
    most = got.at[pl.ds(0, nblk - 1)]
    pltpu.make_async_copy(most, most, recv_sem.at[0]).wait()

    for i in range(here):
        x = got[:, i, :]
        xh, xl = split(jnp.concatenate([x, pltpu.roll(x, chains, 1)], axis=0))
        y = jnp.dot(gram[i], jnp.concatenate([xh, xl], axis=1), preferred_element_type=F32)
        wide, two = 2 * chains, 2 * orders
        y = (y[:two, :wide] + y[:two, wide:]) + (y[two:, :wide] + y[two:, wide:])
        lane_k = lax.broadcasted_iota(I32, (orders, wide), 1)
        stage[:, i, :] = jnp.where(lane_k < chains, y[:orders], y[orders:])
    half[...] = stage[...].astype(BF16)

    @pl.loop(0, nblk - 1)
    def _(t):
        d = other_blk(t)
        pltpu.make_async_remote_copy(
            src_ref=half.at[d], dst_ref=back.at[me], send_sem=send_sem.at[1], recv_sem=recv_sem.at[1],
            device_id=(band, d), device_id_type=MESH,
        ).start()

    pltpu.make_async_copy(half.at[me], back.at[me], own_sem.at[2]).start()

    pltpu.make_async_copy(beam_ref, beams.at[band], own_sem.at[1]).wait()
    pltpu.make_async_copy(beams.at[pl.ds(0, nband - 1)], beams.at[pl.ds(0, nband - 1)], beam_sem.at[1]).wait()
    first = band * rows
    base = first // LANES * LANES
    span = -(-(rows + LANES // 2) // LANES) * LANES
    for b in range(nband):
        line = beams[b, :, pl.ds(pl.multiple_of(base, LANES), span)]
        if rows % LANES:
            line = jnp.where(first - base > 0, pltpu.roll(line, span - LANES // 2, 1), line)
        for g in range(-(-rows // LANES)):
            size = min(LANES, rows - g * LANES)
            block = jnp.broadcast_to(line[:, g * LANES : (g + 1) * LANES], (LANES, LANES)).T
            gains[b, g * LANES : g * LANES + size, :] = block[:size]

    pltpu.make_async_copy(half.at[me], back.at[me], own_sem.at[2]).wait()
    most = back.at[pl.ds(0, nblk - 1)]
    pltpu.make_async_copy(most, most, recv_sem.at[1]).wait()
    got[...] = back[...].astype(F32)
    for i in range(here):
        around[band, i * nblk : (i + 1) * nblk, :] = got[:, i, :].astype(BF16)

    for dx in range(1, nx):
        pltpu.make_async_remote_copy(
            src_ref=around.at[band], dst_ref=around.at[band], send_sem=ag_send.at[dx], recv_sem=ag_recv.at[dx],
            device_id=(band_of(dx, 0), me), device_id_type=MESH,
        ).start()

    def hand_on(dx):
        slot = band_of(-dx, 0)
        return pltpu.make_async_remote_copy(
            src_ref=around.at[slot], dst_ref=around.at[slot], send_sem=fw_send.at[dx], recv_sem=fw_recv.at[dx],
            device_id=(band_of(0, 1), me), device_id_type=MESH,
        )

    def from_chip(dx):
        slot = band_of(-dx, 0)
        return pltpu.make_async_remote_copy(
            src_ref=around.at[slot], dst_ref=around.at[slot], send_sem=ag_send.at[dx], recv_sem=ag_recv.at[dx],
            device_id=(band_of(dx, 0), me), device_id_type=MESH,
        )

    def term(slot):
        return gains[slot] * jnp.dot(legp[...], around[slot], preferred_element_type=F32)

    hand_on(0).start()
    out_ref[...] = term(band)
    arrivals = [1, nx - 1] + list(range(2, nx - 1)) if nx > 2 else list(range(1, nx))
    for dx in arrivals:
        from_chip(dx).wait_recv()
        hand_on(dx).start()
        out_ref[...] += term(band_of(-dx, 0))
    for dx in [0] + arrivals:
        slot = band_of(-dx, 1)
        pltpu.make_async_copy(around.at[slot], around.at[slot], fw_recv.at[dx]).wait()
        out_ref[...] += term(slot)

    for dx in range(1, nx):
        from_chip(dx).wait_send()
    for dx in range(nx):
        hand_on(dx).wait_send()
    for k in range(nband - 1):
        pltpu.make_async_copy(beam_ref, beam_ref, beam_sem.at[0]).wait()
    most = syn.at[pl.ds(0, nblk - 1)]
    pltpu.make_async_copy(most, most, send_sem.at[0]).wait()
    most = half.at[pl.ds(0, nblk - 1)]
    pltpu.make_async_copy(most, most, send_sem.at[1]).wait()


def shards(nband, nblk, amps, beam, legendre, m_values, cycle_order, pixel_counts, inv_noise):
    degrees, _, wide = amps.shape
    cycles = legendre.shape[2]
    orders = m_values.shape[0]
    here = cycles // nblk
    pixels = inv_noise.shape[2]
    rows = degrees // nband
    steps = pixels // WIDE
    vmem = pl.BlockSpec(memory_space=pltpu.VMEM)
    smem = pl.BlockSpec(memory_space=pltpu.SMEM)
    dma = pltpu.SemaphoreType.DMA
    out = pl.pallas_call(
        functools.partial(kernel, nband, nblk),
        out_shape=jax.ShapeDtypeStruct((rows, wide), F32),
        in_specs=[smem, smem, smem, vmem, vmem, vmem, vmem],
        out_specs=vmem,
        scratch_shapes=[
            pltpu.VMEM((orders, LANES), F32),
            pltpu.VMEM((here * steps, orders, LANES), F32),
            pltpu.VMEM((here * steps, orders, LANES), F32),
            pltpu.VMEM((orders, WIDE), F32),
            pltpu.VMEM((orders, WIDE), F32),
            pltpu.VMEM((here, 4 * orders, 2 * orders), BF16),
            pltpu.VMEM((cycles, wide), F32),
            pltpu.VMEM((nblk, here, wide), F32),
            pltpu.VMEM((nblk, here, wide), F32),
            pltpu.VMEM((orders, here, wide), F32),
            pltpu.VMEM((orders, here, wide), BF16),
            pltpu.VMEM((nblk, here, wide), BF16),
            pltpu.VMEM((nband, cycles, wide), BF16),
            pltpu.VMEM((rows, cycles), BF16),
            pltpu.VMEM((nband, 1, degrees), F32),
            pltpu.VMEM((nband, rows, wide), F32),
            pltpu.VMEM((here, 1, pixels), F32),
            dma((2,)),
            dma((2,)),
            dma((3,)),
            dma((2,)),
            dma((nband // 2,)),
            dma((nband // 2,)),
            dma((nband // 2,)),
            dma((nband // 2,)),
        ],
        compiler_params=pltpu.CompilerParams(
            collective_id=0, has_side_effects=True, vmem_limit_bytes=60 * 1024 * 1024
        ),
    )(
        m_values, cycle_order, pixel_counts,
        amps.reshape(degrees, wide), beam, legendre.reshape(degrees, cycles), inv_noise.reshape(here, pixels),
    )
    return out.reshape(rows, 1, wide)


def solution(mesh):
    nband, nblk = mesh.shape["band"], mesh.shape["blk"]
    placed = (
        P(None, "blk", None),
        P("band", None),
        P("blk", None, None),
        P(),
        P(),
        P(),
        P("band", "blk", None),
    )
    return jax.shard_map(
        functools.partial(shards, nband, nblk),
        mesh=mesh, in_specs=placed, out_specs=P("band", "blk", None), check_vma=False,
    )
```

```python
import functools
import math

import jax
import jax.numpy as jnp
from jax import lax
from jax.experimental import pallas as pl
from jax.experimental.pallas import tpu as pltpu
from jax.sharding import PartitionSpec as P

MESH = pl.DeviceIdType.MESH
F32, BF16, I32 = jnp.float32, jnp.bfloat16, jnp.int32
LANES = 128
WIDE = 512
NY = 4


def dot_nt(a, b):
    return lax.dot_general(a, b, (((1,), (1,)), ((), ())), preferred_element_type=F32)


def split(x):
    high = x.astype(BF16)
    return high, (x - high.astype(F32)).astype(BF16)


def remainder(x, count, inverse):
    r = x - jnp.floor(x * inverse) * count
    r = jnp.where(r < 0.0, r + count, r)
    return jnp.where(r >= count, r - count, r)


def turn(doubled, count, inverse):
    k = jnp.floor(doubled * inverse + 0.5)
    phi = (doubled - k * count) * (inverse * jnp.float32(math.pi / 2))
    sq = phi * phi
    sin = phi + phi * sq * (-1.6666654611e-1 + sq * (8.3321608736e-3 + sq * -1.9515295891e-4))
    cos = 1.0 - 0.5 * sq + sq * sq * (
        4.166664568298827e-2 + sq * (-1.388731625493765e-3 + sq * 2.443315711809948e-5)
    )
    ki = k.astype(I32)
    odd = (ki & 1) == 1
    c = jnp.where(odd, sin, cos)
    s = jnp.where(odd, cos, sin)
    return jnp.where(((ki + 1) & 2) != 0, -c, c), jnp.where((ki & 2) != 0, s, -s)


def kernel(
    nband, nblk,
    m_ref, order_ref, counts_ref, amps_ref, beam_ref, leg_ref, noise_ref,
    out_ref,
    m_col, a_cos, a_sin, b_cos, b_sin, gram, flat, syn, got, stage, half, back, around, legp, beams, gains, inside,
    send_sem, recv_sem, own_sem, beam_sem, ag_send, ag_recv, fw_send, fw_recv,
):
    band = lax.axis_index("band")
    me = lax.axis_index("blk")
    nz = nblk // NY
    nx = nband // 2
    degrees = leg_ref.shape[0]
    cycles = leg_ref.shape[1]
    orders = m_col.shape[0]
    here = cycles // nblk
    pixels = noise_ref.shape[1]
    steps = pixels // WIDE
    chains = amps_ref.shape[1] // 2
    rows = degrees // nband
    my_y, my_z = me // nz, me & (nz - 1)
    my_x, core = band // 2, band & 1

    column = [((my_y + k) & (NY - 1)) * nz for k in range(NY)]

    def each_other(act):
        @pl.loop(0, nz - 1)
        def _(u):
            z = (my_z + nz // 2 + ((u >> 1) ^ -(u & 1))) & (nz - 1)
            for k in (2, 1, 3, 0):
                act(column[k] + z)

        for k in (2, 1, 3):
            act(column[k] + my_z)

    def band_of(dx, dc):
        return ((my_x + dx) & (nx - 1)) * 2 + ((core + dc) & 1)

    others = [(dx, dc) for dx in range(nx) for dc in range(2) if (dx, dc) != (0, 0)]

    barrier = pltpu.get_barrier_semaphore()

    each_other(lambda d: pl.semaphore_signal(barrier, inc=1, device_id=(band, d), device_id_type=MESH))

    for dx, dc in others:
        pl.semaphore_signal(barrier, inc=1, device_id=(band_of(dx, dc), me), device_id_type=MESH)

    def synth_step(i, total):
        parts = []
        for h in range(2):
            at = pl.multiple_of(i * 2 * LANES + h * LANES, LANES)
            piece = amps_ref[pl.ds(at, LANES), :].astype(F32).T
            parts.append((piece * beam_ref[:, pl.ds(at, LANES)]).astype(BF16))
        weighted = jnp.concatenate(parts, axis=1)
        at = pl.multiple_of(i * 2 * LANES, LANES)
        return total + jnp.dot(weighted, leg_ref[pl.ds(at, 2 * LANES), :], preferred_element_type=F32)

    total = lax.fori_loop(0, degrees // (2 * LANES), synth_step, jnp.zeros((2 * chains, cycles), F32))
    flat[...] = total.T
    for i in range(here):
        syn[:, i, :] = flat[pl.ds(i, nblk, stride=here), :]

    @pl.loop(0, orders)
    def _(i):
        m_col[pl.ds(i, 1), :] = jnp.full((1, LANES), m_ref[i], I32).astype(F32)

    lane = lax.broadcasted_iota(I32, (1, LANES), 1)

    def cycle(i):
        q = order_ref[me * here + i]
        return counts_ref[q], q & 1

    m = m_col[...]
    count_v = jnp.full((1, LANES), 1, I32)
    parity_v = jnp.zeros((1, LANES), I32)
    pixel = lax.broadcasted_iota(I32, (1, pixels), 1)
    for i in range(here):
        n, parity = cycle(i)
        inside[i] = jnp.where(pixel < n, jnp.sqrt(noise_ref[i : i + 1, :]), 0.0)
        mine = lane // steps == i
        count_v = jnp.where(mine, n, count_v)
        parity_v = jnp.where(mine, parity, parity_v)
    count_v = count_v.astype(F32)
    inverse_v = 1.0 / count_v
    r = remainder(m * ((lane % steps) * WIDE).astype(F32), count_v, inverse_v)
    ca, sa = turn(4.0 * r + 2.0 * m * parity_v.astype(F32), count_v, inverse_v)
    for t in range(here * steps):
        a_cos[t] = jnp.broadcast_to(ca[:, t : t + 1], (orders, LANES))
        a_sin[t] = jnp.broadcast_to(sa[:, t : t + 1], (orders, LANES))

    def form_gram(i):
        n, _ = cycle(i)
        count = jnp.full((1, LANES), n, I32).astype(F32)
        inverse = 1.0 / count
        for g in range(WIDE // LANES):
            r = remainder(m_col[...] * (lane + g * LANES).astype(F32), count, inverse)
            c, s = turn(4.0 * r, count, inverse)
            b_cos[:, g * LANES : (g + 1) * LANES] = c
            b_sin[:, g * LANES : (g + 1) * LANES] = s

        def step(a, acc):
            c1, s1 = a_cos[i * steps + a], a_sin[i * steps + a]
            highs, lows = [], []
            for g in range(WIDE // LANES):
                c2, s2 = b_cos[:, g * LANES : (g + 1) * LANES], b_sin[:, g * LANES : (g + 1) * LANES]
                w = inside[i, :, pl.ds(pl.multiple_of(a * WIDE + g * LANES, LANES), LANES)]
                ch, cl = split((c1 * c2 - s1 * s2) * w)
                sh, sl = split((s1 * c2 + c1 * s2) * w)
                highs.append(jnp.concatenate([ch, sh], axis=0))
                lows.append(jnp.concatenate([cl, sl], axis=0))
            high, low = jnp.concatenate(highs, axis=1), jnp.concatenate(lows, axis=1)
            return acc + dot_nt(high, jnp.concatenate([high, low], axis=0))

        two = 2 * orders
        acc = lax.fori_loop(0, steps, step, jnp.zeros((two, 2 * two), F32))
        cross = acc[:, two:]
        full = acc[:, :two] + (cross + cross.T)
        full = full * inverse[:, :two] if two <= LANES else full * inverse[:, :1]
        full = jnp.concatenate([full[:orders], pltpu.roll(full[orders:], orders, 1)], axis=0)
        gram[i] = jnp.concatenate(split(full), axis=0)

    pl.semaphore_wait(barrier, nblk - 1 + nband - 1)

    def send_to(source, target, k):
        def act(d):
            pltpu.make_async_remote_copy(
                src_ref=source.at[d], dst_ref=target.at[me], send_sem=send_sem.at[k], recv_sem=recv_sem.at[k],
                device_id=(band, d), device_id_type=MESH,
            ).start()

        each_other(act)

    send_to(syn, got, 0)

    pltpu.make_async_copy(syn.at[me], got.at[me], own_sem.at[0]).start()
    for dx, dc in others:
        pltpu.make_async_remote_copy(
            src_ref=beam_ref, dst_ref=beams.at[band], send_sem=beam_sem.at[0], recv_sem=beam_sem.at[1],
            device_id=(band_of(dx, dc), me), device_id_type=MESH,
        ).start()
    pltpu.make_async_copy(beam_ref, beams.at[band], own_sem.at[1]).start()

    @pl.loop(0, here)
    def _(i):
        form_gram(i)

    row = lax.broadcasted_iota(I32, (cycles, cycles), 0)
    col = lax.broadcasted_iota(I32, (cycles, cycles), 1)
    pick = jnp.where(row == here * (col % nblk) + col // nblk, 1.0, 0.0).astype(BF16)
    mine = leg_ref[pl.ds(pl.multiple_of(band * rows, rows & -rows), rows), :]
    legp[...] = jnp.dot(mine, pick, preferred_element_type=F32).astype(BF16)

    pltpu.make_async_copy(syn.at[me], got.at[me], own_sem.at[0]).wait()
    most = got.at[pl.ds(0, nblk - 1)]
    pltpu.make_async_copy(most, most, recv_sem.at[0]).wait()

    for i in range(here):
        x = got[:, i, :]
        xh, xl = split(jnp.concatenate([x, pltpu.roll(x, chains, 1)], axis=0))
        y = jnp.dot(gram[i], jnp.concatenate([xh, xl], axis=1), preferred_element_type=F32)
        wide, two = 2 * chains, 2 * orders
        y = (y[:two, :wide] + y[:two, wide:]) + (y[two:, :wide] + y[two:, wide:])
        lane_k = lax.broadcasted_iota(I32, (orders, wide), 1)
        stage[:, i, :] = jnp.where(lane_k < chains, y[:orders], y[orders:])
    half[...] = stage[...].astype(BF16)

    send_to(half, back, 1)

    pltpu.make_async_copy(half.at[me], back.at[me], own_sem.at[2]).start()

    pltpu.make_async_copy(beam_ref, beams.at[band], own_sem.at[1]).wait()
    pltpu.make_async_copy(beams.at[pl.ds(0, nband - 1)], beams.at[pl.ds(0, nband - 1)], beam_sem.at[1]).wait()
    first = band * rows
    base = first // LANES * LANES
    span = -(-(rows + LANES // 2) // LANES) * LANES
    for b in range(nband):
        line = beams[b, :, pl.ds(pl.multiple_of(base, LANES), span)]
        if rows % LANES:
            line = jnp.where(first - base > 0, pltpu.roll(line, span - LANES // 2, 1), line)
        for g in range(-(-rows // LANES)):
            size = min(LANES, rows - g * LANES)
            block = jnp.broadcast_to(line[:, g * LANES : (g + 1) * LANES], (LANES, LANES)).T
            gains[b, g * LANES : g * LANES + size, :] = block[:size]

    pltpu.make_async_copy(half.at[me], back.at[me], own_sem.at[2]).wait()
    most = back.at[pl.ds(0, nblk - 1)]
    pltpu.make_async_copy(most, most, recv_sem.at[1]).wait()
    got[...] = back[...].astype(F32)
    for i in range(here):
        around[band, i * nblk : (i + 1) * nblk, :] = got[:, i, :].astype(BF16)

    for dx in range(1, nx):
        pltpu.make_async_remote_copy(
            src_ref=around.at[band], dst_ref=around.at[band], send_sem=ag_send.at[dx], recv_sem=ag_recv.at[dx],
            device_id=(band_of(dx, 0), me), device_id_type=MESH,
        ).start()

    def hand_on(dx):
        slot = band_of(-dx, 0)
        return pltpu.make_async_remote_copy(
            src_ref=around.at[slot], dst_ref=around.at[slot], send_sem=fw_send.at[dx], recv_sem=fw_recv.at[dx],
            device_id=(band_of(0, 1), me), device_id_type=MESH,
        )

    def from_chip(dx):
        slot = band_of(-dx, 0)
        return pltpu.make_async_remote_copy(
            src_ref=around.at[slot], dst_ref=around.at[slot], send_sem=ag_send.at[dx], recv_sem=ag_recv.at[dx],
            device_id=(band_of(dx, 0), me), device_id_type=MESH,
        )

    def term(slot):
        return gains[slot] * jnp.dot(legp[...], around[slot], preferred_element_type=F32)

    hand_on(0).start()
    out_ref[...] = term(band)
    arrivals = [1, nx - 1] + list(range(2, nx - 1)) if nx > 2 else list(range(1, nx))
    for dx in arrivals:
        from_chip(dx).wait_recv()
        hand_on(dx).start()
        out_ref[...] += term(band_of(-dx, 0))
    for dx in [0] + arrivals:
        slot = band_of(-dx, 1)
        pltpu.make_async_copy(around.at[slot], around.at[slot], fw_recv.at[dx]).wait()
        out_ref[...] += term(slot)

    for dx in range(1, nx):
        from_chip(dx).wait_send()
    for dx in range(nx):
        hand_on(dx).wait_send()
    for k in range(nband - 1):
        pltpu.make_async_copy(beam_ref, beam_ref, beam_sem.at[0]).wait()
    most = syn.at[pl.ds(0, nblk - 1)]
    pltpu.make_async_copy(most, most, send_sem.at[0]).wait()
    most = half.at[pl.ds(0, nblk - 1)]
    pltpu.make_async_copy(most, most, send_sem.at[1]).wait()


def shards(nband, nblk, amps, beam, legendre, m_values, cycle_order, pixel_counts, inv_noise):
    degrees, _, wide = amps.shape
    cycles = legendre.shape[2]
    orders = m_values.shape[0]
    here = cycles // nblk
    pixels = inv_noise.shape[2]
    rows = degrees // nband
    steps = pixels // WIDE
    vmem = pl.BlockSpec(memory_space=pltpu.VMEM)
    smem = pl.BlockSpec(memory_space=pltpu.SMEM)
    dma = pltpu.SemaphoreType.DMA
    out = pl.pallas_call(
        functools.partial(kernel, nband, nblk),
        out_shape=jax.ShapeDtypeStruct((rows, wide), F32),
        in_specs=[smem, smem, smem, vmem, vmem, vmem, vmem],
        out_specs=vmem,
        scratch_shapes=[
            pltpu.VMEM((orders, LANES), F32),
            pltpu.VMEM((here * steps, orders, LANES), F32),
            pltpu.VMEM((here * steps, orders, LANES), F32),
            pltpu.VMEM((orders, WIDE), F32),
            pltpu.VMEM((orders, WIDE), F32),
            pltpu.VMEM((here, 4 * orders, 2 * orders), BF16),
            pltpu.VMEM((cycles, wide), F32),
            pltpu.VMEM((nblk, here, wide), F32),
            pltpu.VMEM((nblk, here, wide), F32),
            pltpu.VMEM((orders, here, wide), F32),
            pltpu.VMEM((orders, here, wide), BF16),
            pltpu.VMEM((nblk, here, wide), BF16),
            pltpu.VMEM((nband, cycles, wide), BF16),
            pltpu.VMEM((rows, cycles), BF16),
            pltpu.VMEM((nband, 1, degrees), F32),
            pltpu.VMEM((nband, rows, wide), F32),
            pltpu.VMEM((here, 1, pixels), F32),
            dma((2,)),
            dma((2,)),
            dma((3,)),
            dma((2,)),
            dma((nband // 2,)),
            dma((nband // 2,)),
            dma((nband // 2,)),
            dma((nband // 2,)),
        ],
        compiler_params=pltpu.CompilerParams(
            collective_id=0, has_side_effects=True, vmem_limit_bytes=60 * 1024 * 1024
        ),
    )(
        m_values, cycle_order, pixel_counts,
        amps.reshape(degrees, wide), beam, legendre.reshape(degrees, cycles), inv_noise.reshape(here, pixels),
    )
    return out.reshape(rows, 1, wide)


def solution(mesh):
    nband, nblk = mesh.shape["band"], mesh.shape["blk"]
    placed = (
        P(None, "blk", None),
        P("band", None),
        P("blk", None, None),
        P(),
        P(),
        P(),
        P("band", "blk", None),
    )
    return jax.shard_map(
        functools.partial(shards, nband, nblk),
        mesh=mesh, in_specs=placed, out_specs=P("band", "blk", None), check_vma=False,
    )
```

```python
import functools
import math

import jax
import jax.numpy as jnp
from jax import lax
from jax.experimental import pallas as pl
from jax.experimental.pallas import tpu as pltpu
from jax.sharding import PartitionSpec as P

MESH = pl.DeviceIdType.MESH
F32, BF16, I32 = jnp.float32, jnp.bfloat16, jnp.int32
LANES = 128
WIDE = 512
NY = 4
EARLY = 1


def dot_nt(a, b):
    return lax.dot_general(a, b, (((1,), (1,)), ((), ())), preferred_element_type=F32)


def split(x):
    high = x.astype(BF16)
    return high, (x - high.astype(F32)).astype(BF16)


def remainder(x, count, inverse):
    r = x - jnp.floor(x * inverse) * count
    r = jnp.where(r < 0.0, r + count, r)
    return jnp.where(r >= count, r - count, r)


def turn(doubled, count, inverse):
    k = jnp.floor(doubled * inverse + 0.5)
    phi = (doubled - k * count) * (inverse * jnp.float32(math.pi / 2))
    sq = phi * phi
    sin = phi + phi * sq * (-1.6666654611e-1 + sq * (8.3321608736e-3 + sq * -1.9515295891e-4))
    cos = 1.0 - 0.5 * sq + sq * sq * (
        4.166664568298827e-2 + sq * (-1.388731625493765e-3 + sq * 2.443315711809948e-5)
    )
    ki = k.astype(I32)
    odd = (ki & 1) == 1
    c = jnp.where(odd, sin, cos)
    s = jnp.where(odd, cos, sin)
    return jnp.where(((ki + 1) & 2) != 0, -c, c), jnp.where((ki & 2) != 0, s, -s)


def kernel(
    nband, nblk,
    m_ref, order_ref, counts_ref, beam_ref, amps_in, leg_in, noise_in,
    out_ref, rest_ref,
    amps_ref, leg_ref, noise_ref, in_sem,
    m_col, a_cos, a_sin, b_cos, b_sin, gram, flat, syn, got, stage, half, back, around, legp, beams, gains, inside,
    send_sem, recv_sem, own_sem, beam_sem, ag_send, ag_recv, fw_send, fw_recv,
):
    band = lax.axis_index("band")
    me = lax.axis_index("blk")
    nz = nblk // NY
    nx = nband // 2
    degrees = leg_ref.shape[0]
    cycles = leg_ref.shape[1]
    orders = m_col.shape[0]
    here = cycles // nblk
    pixels = noise_ref.shape[1]
    steps = pixels // WIDE
    chains = amps_ref.shape[1] // 2
    rows = degrees // nband
    my_y, my_z = me // nz, me & (nz - 1)
    my_x, core = band // 2, band & 1

    column = [((my_y + k) & (NY - 1)) * nz for k in range(NY)]

    turns = (2, 1, 3, 0)

    def each_other(act, first, last):
        @pl.loop(first, min(last, nz - 1))
        def _(u):
            z = (my_z + nz // 2 + ((u >> 1) ^ -(u & 1))) & (nz - 1)
            for j, k in enumerate(turns):
                act(column[k] + z, u * NY + j)

        if last == nz:
            for j, k in enumerate(turns[:-1]):
                act(column[k] + my_z, (nz - 1) * NY + j)

    def band_of(dx, dc):
        return ((my_x + dx) & (nx - 1)) * 2 + ((core + dc) & 1)

    others = [(dx, dc) for dx in range(nx) for dc in range(2) if (dx, dc) != (0, 0)]

    barrier = pltpu.get_barrier_semaphore()

    loads = [
        pltpu.make_async_copy(source, target, in_sem.at[k])
        for k, (source, target) in enumerate(((amps_in, amps_ref), (leg_in, leg_ref), (noise_in, noise_ref)))
    ]
    for load in loads:
        load.start()

    each_other(lambda d, t: pl.semaphore_signal(barrier, inc=1, device_id=(band, d), device_id_type=MESH), 0, nz)

    for dx, dc in others:
        pl.semaphore_signal(barrier, inc=1, device_id=(band_of(dx, dc), me), device_id_type=MESH)

    for load in loads:
        load.wait()

    def synth_step(i, total):
        parts = []
        for h in range(2):
            at = pl.multiple_of(i * 2 * LANES + h * LANES, LANES)
            piece = amps_ref[pl.ds(at, LANES), :].astype(F32).T
            parts.append((piece * beam_ref[:, pl.ds(at, LANES)]).astype(BF16))
        weighted = jnp.concatenate(parts, axis=1)
        at = pl.multiple_of(i * 2 * LANES, LANES)
        return total + jnp.dot(weighted, leg_ref[pl.ds(at, 2 * LANES), :], preferred_element_type=F32)

    total = lax.fori_loop(0, degrees // (2 * LANES), synth_step, jnp.zeros((2 * chains, cycles), F32))
    flat[...] = total.T
    for i in range(here):
        syn[:, i, :] = flat[pl.ds(i, nblk, stride=here), :]

    @pl.loop(0, orders, unroll=8)
    def _(i):
        m_col[pl.ds(i, 1), :] = jnp.full((1, LANES), m_ref[i], I32).astype(F32)

    lane = lax.broadcasted_iota(I32, (1, LANES), 1)

    def cycle(i):
        q = order_ref[me * here + i]
        return counts_ref[q], q & 1

    m = m_col[...]
    count_v = jnp.full((1, LANES), 1, I32)
    parity_v = jnp.zeros((1, LANES), I32)
    pixel = lax.broadcasted_iota(I32, (1, pixels), 1)
    for i in range(here):
        n, parity = cycle(i)
        inside[i] = jnp.where(pixel < n, jnp.sqrt(noise_ref[i : i + 1, :]), 0.0)
        mine = lane // 16 == i
        count_v = jnp.where(mine, n, count_v)
        parity_v = jnp.where(mine, parity, parity_v)
    count_v = count_v.astype(F32)
    inverse_v = 1.0 / count_v
    entry = lane % 16
    coarse = entry < steps
    stride = jnp.where(coarse, entry * WIDE, (entry - steps) * LANES)
    parity_v = jnp.where(coarse, parity_v, 0)
    r = remainder(m * stride.astype(F32), count_v, inverse_v)
    ca, sa = turn(4.0 * r + 2.0 * m * parity_v.astype(F32), count_v, inverse_v)
    kinds = steps + WIDE // LANES
    for i in range(here):
        for e in range(kinds):
            t = i * 16 + e
            a_cos[i * kinds + e] = jnp.broadcast_to(ca[:, t : t + 1], (orders, LANES))
            a_sin[i * kinds + e] = jnp.broadcast_to(sa[:, t : t + 1], (orders, LANES))

    def form_gram(i):
        n, _ = cycle(i)
        count = jnp.full((1, LANES), n, I32).astype(F32)
        inverse = 1.0 / count
        r = remainder(m_col[...] * lane.astype(F32), count, inverse)
        c2, s2 = turn(4.0 * r, count, inverse)
        b_cos[:, :LANES], b_sin[:, :LANES] = c2, s2
        for g in range(1, WIDE // LANES):
            c1, s1 = a_cos[i * kinds + steps + g], a_sin[i * kinds + steps + g]
            b_cos[:, g * LANES : (g + 1) * LANES] = c1 * c2 - s1 * s2
            b_sin[:, g * LANES : (g + 1) * LANES] = s1 * c2 + c1 * s2

        def step(a, acc):
            c1, s1 = a_cos[i * kinds + a], a_sin[i * kinds + a]
            highs, lows = [], []
            for g in range(WIDE // LANES):
                c2, s2 = b_cos[:, g * LANES : (g + 1) * LANES], b_sin[:, g * LANES : (g + 1) * LANES]
                w = inside[i, :, pl.ds(pl.multiple_of(a * WIDE + g * LANES, LANES), LANES)]
                ch, cl = split((c1 * c2 - s1 * s2) * w)
                sh, sl = split((s1 * c2 + c1 * s2) * w)
                highs.append(jnp.concatenate([ch, sh], axis=0))
                lows.append(jnp.concatenate([cl, sl], axis=0))
            high, low = jnp.concatenate(highs, axis=1), jnp.concatenate(lows, axis=1)
            return acc + dot_nt(high, jnp.concatenate([high, low], axis=0))

        two = 2 * orders
        acc = lax.fori_loop(0, steps, step, jnp.zeros((two, 2 * two), F32))
        cross = acc[:, two:]
        full = acc[:, :two] + (cross + cross.T)
        full = full * inverse[:, :two] if two <= LANES else full * inverse[:, :1]
        full = jnp.concatenate([full[:orders], pltpu.roll(full[orders:], orders, 1)], axis=0)
        gram[i] = jnp.concatenate(split(full), axis=0)

    @pl.loop(0, EARLY)
    def _(i):
        form_gram(i)

    pl.semaphore_wait(barrier, nblk - 1 + nband - 1)

    def send(d, t):
        pltpu.make_async_remote_copy(
            src_ref=syn.at[d], dst_ref=got.at[me], send_sem=send_sem.at[0], recv_sem=recv_sem.at[0],
            device_id=(band, d), device_id_type=MESH,
        ).start()

    each_other(send, 0, nz)
    pltpu.make_async_copy(syn.at[me], got.at[me], own_sem.at[0]).start()
    for dx, dc in others:
        pltpu.make_async_remote_copy(
            src_ref=beam_ref, dst_ref=beams.at[band], send_sem=beam_sem.at[0], recv_sem=beam_sem.at[1],
            device_id=(band_of(dx, dc), me), device_id_type=MESH,
        ).start()
    pltpu.make_async_copy(beam_ref, beams.at[band], own_sem.at[1]).start()

    @pl.loop(EARLY, here)
    def _(i):
        form_gram(i)

    row = lax.broadcasted_iota(I32, (cycles, cycles), 0)
    col = lax.broadcasted_iota(I32, (cycles, cycles), 1)
    slot = col % (nblk // 2) + col // (cycles // 2) * (nblk // 2)
    u, j = slot // NY, slot % NY
    k = jnp.where(j == 3, 0, jnp.where(j == 2, 3, 2 - j))
    z = (my_z - nz // 2 - ((u >> 1) ^ -(u & 1))) & (nz - 1)
    source = ((my_y - k) & (NY - 1)) * nz + z
    pick = jnp.where(row == here * source + col // (nblk // 2) % here, 1.0, 0.0).astype(BF16)
    mine = leg_ref[pl.ds(pl.multiple_of(band * rows, rows & -rows), rows), :]
    legp[...] = jnp.dot(mine, pick, preferred_element_type=F32).astype(BF16)

    pltpu.make_async_copy(syn.at[me], got.at[me], own_sem.at[0]).wait()
    most = got.at[pl.ds(0, nblk - 1)]
    pltpu.make_async_copy(most, most, recv_sem.at[0]).wait()

    for i in range(here):
        x = got[:, i, :]
        xh, xl = split(jnp.concatenate([x, pltpu.roll(x, chains, 1)], axis=0))
        y = jnp.dot(gram[i], jnp.concatenate([xh, xl], axis=1), preferred_element_type=F32)
        wide, two = 2 * chains, 2 * orders
        y = (y[:two, :wide] + y[:two, wide:]) + (y[two:, :wide] + y[two:, wide:])
        lane_k = lax.broadcasted_iota(I32, (orders, wide), 1)
        stage[:, i, :] = jnp.where(lane_k < chains, y[:orders], y[orders:])
    half[...] = stage[...].astype(BF16)

    for g in range(2):

        def send(d, t, g=g):
            pltpu.make_async_remote_copy(
                src_ref=half.at[d], dst_ref=back.at[t], send_sem=send_sem.at[1], recv_sem=recv_sem.at[1 + g],
                device_id=(band, d), device_id_type=MESH,
            ).start()

        each_other(send, g * nz // 2, (g + 1) * nz // 2)

    pltpu.make_async_copy(half.at[me], back.at[nblk - 1], own_sem.at[2]).start()

    pltpu.make_async_copy(beam_ref, beams.at[band], own_sem.at[1]).wait()
    pltpu.make_async_copy(beams.at[pl.ds(0, nband - 1)], beams.at[pl.ds(0, nband - 1)], beam_sem.at[1]).wait()
    first = band * rows
    base = first // LANES * LANES
    span = -(-(rows + LANES // 2) // LANES) * LANES
    for b in range(nband):
        line = beams[b, :, pl.ds(pl.multiple_of(base, LANES), span)]
        if rows % LANES:
            line = jnp.where(first - base > 0, pltpu.roll(line, span - LANES // 2, 1), line)
        for g in range(-(-rows // LANES)):
            size = min(LANES, rows - g * LANES)
            block = jnp.broadcast_to(line[:, g * LANES : (g + 1) * LANES], (LANES, LANES)).T
            gains[b, g * LANES : g * LANES + size, :] = block[:size]

    per = cycles // 2

    def across(dx, g):
        part = around.at[band, pl.ds(g * per, per)]
        return pltpu.make_async_remote_copy(
            src_ref=part, dst_ref=part, send_sem=ag_send.at[g * nx + dx], recv_sem=ag_recv.at[g * nx + dx],
            device_id=(band_of(dx, 0), me), device_id_type=MESH,
        )

    def arrival(sem, dx, dc, g):
        part = around.at[band_of(-dx, dc), pl.ds(g * per, per)]
        return pltpu.make_async_copy(part, part, sem.at[g * nx + dx])

    def hand_on(dx, g):
        part = around.at[band_of(-dx, 0), pl.ds(g * per, per)]
        return pltpu.make_async_remote_copy(
            src_ref=part, dst_ref=part, send_sem=fw_send.at[g * nx + dx], recv_sem=fw_recv.at[g * nx + dx],
            device_id=(band_of(0, 1), me), device_id_type=MESH,
        )

    hops = [nx // 2] + [dx for dx in range(1, nx) if dx != nx // 2]
    for g in (1, 0):
        lot = nblk // 2
        if g == 1:
            pltpu.make_async_copy(half.at[me], back.at[nblk - 1], own_sem.at[2]).wait()
        most = back.at[pl.ds(g * lot, lot - g)]
        pltpu.make_async_copy(most, most, recv_sem.at[1 + g]).wait()
        stage[g * lot : (g + 1) * lot] = back[g * lot : (g + 1) * lot].astype(F32)
        for i in range(here):
            at = g * per + i * lot
            around[band, at : at + lot, :] = stage[g * lot : (g + 1) * lot, i, :].astype(BF16)
        for dx in hops:
            across(dx, g).start()
        hand_on(0, g).start()

    ready = hops[1:] + hops[:1]
    for g in (1, 0):
        for dx in ready:
            arrival(ag_recv, dx, 0, g).wait()
            hand_on(dx, g).start()

    def terms(slots):
        total = None
        for slot in slots:
            one = gains[slot] * jnp.dot(legp[...], around[slot], preferred_element_type=F32)
            total = one if total is None else total + one
        return total

    for g in (1, 0):
        arrival(fw_recv, 0, 1, g).wait()
    out_ref[...] = terms([band_of(-dx, 0) for dx in range(nx)] + [band_of(0, 1)])
    for g in (1, 0):
        for dx in ready:
            arrival(fw_recv, dx, 1, g).wait()
    rest_ref[...] = terms([band_of(-dx, 1) for dx in ready])

    for g in (1, 0):
        for dx in hops:
            across(dx, g).wait_send()
        for dx in range(nx):
            hand_on(dx, g).wait_send()
    for k in range(nband - 1):
        pltpu.make_async_copy(beam_ref, beam_ref, beam_sem.at[0]).wait()
    most = syn.at[pl.ds(0, nblk - 1)]
    pltpu.make_async_copy(most, most, send_sem.at[0]).wait()
    most = half.at[pl.ds(0, nblk - 1)]
    pltpu.make_async_copy(most, most, send_sem.at[1]).wait()


def shards(nband, nblk, amps, beam, legendre, m_values, cycle_order, pixel_counts, inv_noise):
    degrees, _, wide = amps.shape
    cycles = legendre.shape[2]
    orders = m_values.shape[0]
    here = cycles // nblk
    pixels = inv_noise.shape[2]
    rows = degrees // nband
    steps = pixels // WIDE
    vmem = pl.BlockSpec(memory_space=pltpu.VMEM)
    left = pl.BlockSpec(memory_space=pl.ANY)
    smem = pl.BlockSpec(memory_space=pltpu.SMEM)
    dma = pltpu.SemaphoreType.DMA
    most, rest = pl.pallas_call(
        functools.partial(kernel, nband, nblk),
        out_shape=[jax.ShapeDtypeStruct((rows, wide), F32)] * 2,
        in_specs=[smem, smem, smem, vmem, left, left, left],
        out_specs=[vmem, vmem],
        scratch_shapes=[
            pltpu.VMEM((degrees, wide), BF16),
            pltpu.VMEM((degrees, cycles), BF16),
            pltpu.VMEM((here, pixels), F32),
            dma((3,)),
            pltpu.VMEM((orders, LANES), F32),
            pltpu.VMEM((here * (steps + WIDE // LANES), orders, LANES), F32),
            pltpu.VMEM((here * (steps + WIDE // LANES), orders, LANES), F32),
            pltpu.VMEM((orders, WIDE), F32),
            pltpu.VMEM((orders, WIDE), F32),
            pltpu.VMEM((here, 4 * orders, 2 * orders), BF16),
            pltpu.VMEM((cycles, wide), F32),
            pltpu.VMEM((nblk, here, wide), F32),
            pltpu.VMEM((nblk, here, wide), F32),
            pltpu.VMEM((orders, here, wide), F32),
            pltpu.VMEM((orders, here, wide), BF16),
            pltpu.VMEM((nblk, here, wide), BF16),
            pltpu.VMEM((nband, cycles, wide), BF16),
            pltpu.VMEM((rows, cycles), BF16),
            pltpu.VMEM((nband, 1, degrees), F32),
            pltpu.VMEM((nband, rows, wide), F32),
            pltpu.VMEM((here, 1, pixels), F32),
            dma((2,)),
            dma((3,)),
            dma((3,)),
            dma((2,)),
            dma((nband,)),
            dma((nband,)),
            dma((nband,)),
            dma((nband,)),
        ],
        compiler_params=pltpu.CompilerParams(
            collective_id=0, has_side_effects=True, vmem_limit_bytes=60 * 1024 * 1024
        ),
    )(
        m_values, cycle_order, pixel_counts,
        beam, amps.reshape(degrees, wide), legendre.reshape(degrees, cycles), inv_noise.reshape(here, pixels),
    )
    return (most + rest).reshape(rows, 1, wide)


def solution(mesh):
    nband, nblk = mesh.shape["band"], mesh.shape["blk"]
    placed = (
        P(None, "blk", None),
        P("band", None),
        P("blk", None, None),
        P(),
        P(),
        P(),
        P("band", "blk", None),
    )
    return jax.shard_map(
        functools.partial(shards, nband, nblk),
        mesh=mesh, in_specs=placed, out_specs=P("band", "blk", None), check_vma=False,
    )
```

```python
import functools
import math

import jax
import jax.numpy as jnp
from jax import lax
from jax.experimental import pallas as pl
from jax.experimental.pallas import tpu as pltpu
from jax.sharding import PartitionSpec as P

MESH = pl.DeviceIdType.MESH
F32, BF16, I32 = jnp.float32, jnp.bfloat16, jnp.int32
LANES = 128
WIDE = 512
NY = 4
EARLY = 1


def dot_nt(a, b):
    return lax.dot_general(a, b, (((1,), (1,)), ((), ())), preferred_element_type=F32)


def split(x):
    high = x.astype(BF16)
    return high, (x - high.astype(F32)).astype(BF16)


def remainder(x, count, inverse):
    r = x - jnp.floor(x * inverse) * count
    r = jnp.where(r < 0.0, r + count, r)
    return jnp.where(r >= count, r - count, r)


def turn(doubled, count, inverse):
    k = jnp.floor(doubled * inverse + 0.5)
    phi = (doubled - k * count) * (inverse * jnp.float32(math.pi / 2))
    sq = phi * phi
    sin = phi + phi * sq * (-1.6666654611e-1 + sq * (8.3321608736e-3 + sq * -1.9515295891e-4))
    cos = 1.0 - 0.5 * sq + sq * sq * (
        4.166664568298827e-2 + sq * (-1.388731625493765e-3 + sq * 2.443315711809948e-5)
    )
    ki = k.astype(I32)
    odd = (ki & 1) == 1
    c = jnp.where(odd, sin, cos)
    s = jnp.where(odd, cos, sin)
    return jnp.where(((ki + 1) & 2) != 0, -c, c), jnp.where((ki & 2) != 0, s, -s)


def kernel(
    nband, nblk,
    m_ref, order_ref, counts_ref, beam_ref, amps_in, leg_in, noise_in,
    out_ref, rest_ref,
    amps_ref, leg_ref, noise_ref, in_sem,
    m_col, a_cos, a_sin, b_cos, b_sin, gram, flat, syn, got, stage, half, back, around, legp, beams, gains, inside,
    send_sem, recv_sem, own_sem, beam_sem, ag_send, ag_recv,
):
    band = lax.axis_index("band")
    me = lax.axis_index("blk")
    nz = nblk // NY
    nx = nband // 2
    degrees = leg_ref.shape[0]
    cycles = leg_ref.shape[1]
    orders = m_col.shape[0]
    here = cycles // nblk
    pixels = noise_ref.shape[1]
    steps = pixels // WIDE
    chains = amps_ref.shape[1] // 2
    rows = degrees // nband
    my_y, my_z = me // nz, me & (nz - 1)
    my_x, core = band // 2, band & 1

    column = [((my_y + k) & (NY - 1)) * nz for k in range(NY)]

    turns = (2, 1, 3, 0)

    def each_other(act, first, last):
        @pl.loop(first, min(last, nz - 1))
        def _(u):
            z = (my_z + nz // 2 + ((u >> 1) ^ -(u & 1))) & (nz - 1)
            for j, k in enumerate(turns):
                act(column[k] + z, u * NY + j)

        if last == nz:
            for j, k in enumerate(turns[:-1]):
                act(column[k] + my_z, (nz - 1) * NY + j)

    def band_of(dx, dc):
        return ((my_x + dx) & (nx - 1)) * 2 + ((core + dc) & 1)

    others = [(dx, dc) for dx in range(nx) for dc in range(2) if (dx, dc) != (0, 0)]

    barrier = pltpu.get_barrier_semaphore()

    loads = [
        pltpu.make_async_copy(source, target, in_sem.at[k])
        for k, (source, target) in enumerate(((amps_in, amps_ref), (leg_in, leg_ref), (noise_in, noise_ref)))
    ]
    for load in loads:
        load.start()

    each_other(lambda d, t: pl.semaphore_signal(barrier, inc=1, device_id=(band, d), device_id_type=MESH), 0, nz)

    for dx, dc in others:
        pl.semaphore_signal(barrier, inc=1, device_id=(band_of(dx, dc), me), device_id_type=MESH)

    for load in loads:
        load.wait()

    def synth_step(i, total):
        parts = []
        for h in range(2):
            at = pl.multiple_of(i * 2 * LANES + h * LANES, LANES)
            piece = amps_ref[pl.ds(at, LANES), :].astype(F32).T
            parts.append((piece * beam_ref[:, pl.ds(at, LANES)]).astype(BF16))
        weighted = jnp.concatenate(parts, axis=1)
        at = pl.multiple_of(i * 2 * LANES, LANES)
        return total + jnp.dot(weighted, leg_ref[pl.ds(at, 2 * LANES), :], preferred_element_type=F32)

    total = lax.fori_loop(0, degrees // (2 * LANES), synth_step, jnp.zeros((2 * chains, cycles), F32))
    flat[...] = total.T
    for i in range(here):
        syn[:, i, :] = flat[pl.ds(i, nblk, stride=here), :]

    @pl.loop(0, orders, unroll=8)
    def _(i):
        m_col[pl.ds(i, 1), :] = jnp.full((1, LANES), m_ref[i], I32).astype(F32)

    lane = lax.broadcasted_iota(I32, (1, LANES), 1)

    def cycle(i):
        q = order_ref[me * here + i]
        return counts_ref[q], q & 1

    m = m_col[...]
    count_v = jnp.full((1, LANES), 1, I32)
    parity_v = jnp.zeros((1, LANES), I32)
    pixel = lax.broadcasted_iota(I32, (1, pixels), 1)
    for i in range(here):
        n, parity = cycle(i)
        inside[i] = jnp.where(pixel < n, jnp.sqrt(noise_ref[i : i + 1, :]), 0.0)
        mine = lane // 16 == i
        count_v = jnp.where(mine, n, count_v)
        parity_v = jnp.where(mine, parity, parity_v)
    count_v = count_v.astype(F32)
    inverse_v = 1.0 / count_v
    entry = lane % 16
    coarse = entry < steps
    stride = jnp.where(coarse, entry * WIDE, (entry - steps) * LANES)
    parity_v = jnp.where(coarse, parity_v, 0)
    r = remainder(m * stride.astype(F32), count_v, inverse_v)
    ca, sa = turn(4.0 * r + 2.0 * m * parity_v.astype(F32), count_v, inverse_v)
    kinds = steps + WIDE // LANES
    for i in range(here):
        for e in range(kinds):
            t = i * 16 + e
            a_cos[i * kinds + e] = jnp.broadcast_to(ca[:, t : t + 1], (orders, LANES))
            a_sin[i * kinds + e] = jnp.broadcast_to(sa[:, t : t + 1], (orders, LANES))

    def form_gram(i):
        n, _ = cycle(i)
        count = jnp.full((1, LANES), n, I32).astype(F32)
        inverse = 1.0 / count
        r = remainder(m_col[...] * lane.astype(F32), count, inverse)
        c2, s2 = turn(4.0 * r, count, inverse)
        b_cos[:, :LANES], b_sin[:, :LANES] = c2, s2
        for g in range(1, WIDE // LANES):
            c1, s1 = a_cos[i * kinds + steps + g], a_sin[i * kinds + steps + g]
            b_cos[:, g * LANES : (g + 1) * LANES] = c1 * c2 - s1 * s2
            b_sin[:, g * LANES : (g + 1) * LANES] = s1 * c2 + c1 * s2

        def step(a, acc):
            c1, s1 = a_cos[i * kinds + a], a_sin[i * kinds + a]
            highs, lows = [], []
            for g in range(WIDE // LANES):
                c2, s2 = b_cos[:, g * LANES : (g + 1) * LANES], b_sin[:, g * LANES : (g + 1) * LANES]
                w = inside[i, :, pl.ds(pl.multiple_of(a * WIDE + g * LANES, LANES), LANES)]
                ch, cl = split((c1 * c2 - s1 * s2) * w)
                sh, sl = split((s1 * c2 + c1 * s2) * w)
                highs.append(jnp.concatenate([ch, sh], axis=0))
                lows.append(jnp.concatenate([cl, sl], axis=0))
            high, low = jnp.concatenate(highs, axis=1), jnp.concatenate(lows, axis=1)
            return acc + dot_nt(high, jnp.concatenate([high, low], axis=0))

        two = 2 * orders
        acc = lax.fori_loop(0, steps, step, jnp.zeros((two, 2 * two), F32))
        cross = acc[:, two:]
        full = acc[:, :two] + (cross + cross.T)
        full = full * inverse[:, :two] if two <= LANES else full * inverse[:, :1]
        full = jnp.concatenate([full[:orders], pltpu.roll(full[orders:], orders, 1)], axis=0)
        gram[i] = jnp.concatenate(split(full), axis=0)

    @pl.loop(0, EARLY)
    def _(i):
        form_gram(i)

    pl.semaphore_wait(barrier, nblk - 1 + nband - 1)

    def send(d, t):
        pltpu.make_async_remote_copy(
            src_ref=syn.at[d], dst_ref=got.at[me], send_sem=send_sem.at[0], recv_sem=recv_sem.at[0],
            device_id=(band, d), device_id_type=MESH,
        ).start()

    each_other(send, 0, nz)
    pltpu.make_async_copy(syn.at[me], got.at[me], own_sem.at[0]).start()
    for dx, dc in others:
        pltpu.make_async_remote_copy(
            src_ref=beam_ref, dst_ref=beams.at[band], send_sem=beam_sem.at[0], recv_sem=beam_sem.at[1],
            device_id=(band_of(dx, dc), me), device_id_type=MESH,
        ).start()
    pltpu.make_async_copy(beam_ref, beams.at[band], own_sem.at[1]).start()

    @pl.loop(EARLY, here)
    def _(i):
        form_gram(i)

    row = lax.broadcasted_iota(I32, (cycles, cycles), 0)
    col = lax.broadcasted_iota(I32, (cycles, cycles), 1)
    slot = col % (nblk // 2) + col // (cycles // 2) * (nblk // 2)
    u, j = slot // NY, slot % NY
    k = jnp.where(j == 3, 0, jnp.where(j == 2, 3, 2 - j))
    z = (my_z - nz // 2 - ((u >> 1) ^ -(u & 1))) & (nz - 1)
    source = ((my_y - k) & (NY - 1)) * nz + z
    pick = jnp.where(row == here * source + col // (nblk // 2) % here, 1.0, 0.0).astype(BF16)
    mine = leg_ref[pl.ds(pl.multiple_of(band * rows, rows & -rows), rows), :]
    legp[...] = jnp.dot(mine, pick, preferred_element_type=F32).astype(BF16)

    pltpu.make_async_copy(syn.at[me], got.at[me], own_sem.at[0]).wait()
    most = got.at[pl.ds(0, nblk - 1)]
    pltpu.make_async_copy(most, most, recv_sem.at[0]).wait()

    for i in range(here):
        x = got[:, i, :]
        xh, xl = split(jnp.concatenate([x, pltpu.roll(x, chains, 1)], axis=0))
        y = jnp.dot(gram[i], jnp.concatenate([xh, xl], axis=1), preferred_element_type=F32)
        wide, two = 2 * chains, 2 * orders
        y = (y[:two, :wide] + y[:two, wide:]) + (y[two:, :wide] + y[two:, wide:])
        lane_k = lax.broadcasted_iota(I32, (orders, wide), 1)
        stage[:, i, :] = jnp.where(lane_k < chains, y[:orders], y[orders:])
    half[...] = stage[...].astype(BF16)

    for g in range(2):

        def send(d, t, g=g):
            pltpu.make_async_remote_copy(
                src_ref=half.at[d], dst_ref=back.at[t], send_sem=send_sem.at[1], recv_sem=recv_sem.at[1 + g],
                device_id=(band, d), device_id_type=MESH,
            ).start()

        each_other(send, g * nz // 2, (g + 1) * nz // 2)

    pltpu.make_async_copy(half.at[me], back.at[nblk - 1], own_sem.at[2]).start()

    pltpu.make_async_copy(beam_ref, beams.at[band], own_sem.at[1]).wait()
    pltpu.make_async_copy(beams.at[pl.ds(0, nband - 1)], beams.at[pl.ds(0, nband - 1)], beam_sem.at[1]).wait()
    first = band * rows
    base = first // LANES * LANES
    span = -(-(rows + LANES // 2) // LANES) * LANES
    for b in range(nband):
        line = beams[b, :, pl.ds(pl.multiple_of(base, LANES), span)]
        if rows % LANES:
            line = jnp.where(first - base > 0, pltpu.roll(line, span - LANES // 2, 1), line)
        for g in range(-(-rows // LANES)):
            size = min(LANES, rows - g * LANES)
            block = jnp.broadcast_to(line[:, g * LANES : (g + 1) * LANES], (LANES, LANES)).T
            gains[b, g * LANES : g * LANES + size, :] = block[:size]

    per = cycles // 2

    def across(dx, dc, g):
        part = around.at[band, pl.ds(g * per, per)]
        k = (g * nx + dx) * 2 + dc
        return pltpu.make_async_remote_copy(
            src_ref=part, dst_ref=part, send_sem=ag_send.at[k], recv_sem=ag_recv.at[k],
            device_id=(band_of(dx, dc), me), device_id_type=MESH,
        )

    def arrived(dx, dc, g):
        part = around.at[band_of(-dx, dc), pl.ds(g * per, per)]
        pltpu.make_async_copy(part, part, ag_recv.at[(g * nx + dx) * 2 + dc]).wait()

    far = nx // 2
    near = [dx for dx in range(1, nx) if dx != far]
    direct = [(far, 0), (far, 1), (0, 1)] + [(dx, dc) for dc in range(2) for dx in near]
    for g in (1, 0):
        lot = nblk // 2
        if g == 1:
            pltpu.make_async_copy(half.at[me], back.at[nblk - 1], own_sem.at[2]).wait()
        most = back.at[pl.ds(g * lot, lot - g)]
        pltpu.make_async_copy(most, most, recv_sem.at[1 + g]).wait()
        stage[g * lot : (g + 1) * lot] = back[g * lot : (g + 1) * lot].astype(F32)
        for i in range(here):
            at = g * per + i * lot
            around[band, at : at + lot, :] = stage[g * lot : (g + 1) * lot, i, :].astype(BF16)
        for dx, dc in direct:
            across(dx, dc, g).start()

    def terms(slots):
        total = None
        for i in range(0, len(slots), 2):
            pair = slots[i : i + 2]
            side = jnp.concatenate([around[slot] for slot in pair], axis=1) if len(pair) == 2 else around[pair[0]]
            both = jnp.dot(legp[...], side, preferred_element_type=F32)
            wide = 2 * chains
            for j, slot in enumerate(pair):
                one = gains[slot] * both[:, j * wide : (j + 1) * wide]
                total = one if total is None else total + one
        return total

    for g in (1, 0):
        arrived(0, 1, g)
        arrived(far, 0, g)
        for dx in near:
            arrived(dx, 0, g)
    out_ref[...] = terms([band, band_of(0, 1), band_of(-far, 0)] + [band_of(-dx, 0) for dx in near[:1]])
    for g in (1, 0):
        for dx in near:
            arrived(dx, 1, g)
        arrived(far, 1, g)
    rest_ref[...] = terms([band_of(-dx, 0) for dx in near[1:]] + [band_of(-dx, 1) for dx in near] + [band_of(-far, 1)])

    for g in (1, 0):
        for dx, dc in direct:
            across(dx, dc, g).wait_send()
    for k in range(nband - 1):
        pltpu.make_async_copy(beam_ref, beam_ref, beam_sem.at[0]).wait()
    most = syn.at[pl.ds(0, nblk - 1)]
    pltpu.make_async_copy(most, most, send_sem.at[0]).wait()
    most = half.at[pl.ds(0, nblk - 1)]
    pltpu.make_async_copy(most, most, send_sem.at[1]).wait()


def shards(nband, nblk, amps, beam, legendre, m_values, cycle_order, pixel_counts, inv_noise):
    degrees, _, wide = amps.shape
    cycles = legendre.shape[2]
    orders = m_values.shape[0]
    here = cycles // nblk
    pixels = inv_noise.shape[2]
    rows = degrees // nband
    steps = pixels // WIDE
    vmem = pl.BlockSpec(memory_space=pltpu.VMEM)
    left = pl.BlockSpec(memory_space=pl.ANY)
    smem = pl.BlockSpec(memory_space=pltpu.SMEM)
    dma = pltpu.SemaphoreType.DMA
    most, rest = pl.pallas_call(
        functools.partial(kernel, nband, nblk),
        out_shape=[pltpu.VMEM((rows, wide), F32)] * 2,
        in_specs=[smem, smem, smem, vmem, left, left, left],
        out_specs=[vmem, vmem],
        scratch_shapes=[
            pltpu.VMEM((degrees, wide), BF16),
            pltpu.VMEM((degrees, cycles), BF16),
            pltpu.VMEM((here, pixels), F32),
            dma((3,)),
            pltpu.VMEM((orders, LANES), F32),
            pltpu.VMEM((here * (steps + WIDE // LANES), orders, LANES), F32),
            pltpu.VMEM((here * (steps + WIDE // LANES), orders, LANES), F32),
            pltpu.VMEM((orders, WIDE), F32),
            pltpu.VMEM((orders, WIDE), F32),
            pltpu.VMEM((here, 4 * orders, 2 * orders), BF16),
            pltpu.VMEM((cycles, wide), F32),
            pltpu.VMEM((nblk, here, wide), F32),
            pltpu.VMEM((nblk, here, wide), F32),
            pltpu.VMEM((orders, here, wide), F32),
            pltpu.VMEM((orders, here, wide), BF16),
            pltpu.VMEM((nblk, here, wide), BF16),
            pltpu.VMEM((nband, cycles, wide), BF16),
            pltpu.VMEM((rows, cycles), BF16),
            pltpu.VMEM((nband, 1, degrees), F32),
            pltpu.VMEM((nband, rows, wide), F32),
            pltpu.VMEM((here, 1, pixels), F32),
            dma((2,)),
            dma((3,)),
            dma((3,)),
            dma((2,)),
            dma((2 * nband,)),
            dma((2 * nband,)),
        ],
        compiler_params=pltpu.CompilerParams(
            collective_id=0, has_side_effects=True, vmem_limit_bytes=60 * 1024 * 1024
        ),
    )(
        m_values, cycle_order, pixel_counts,
        beam, amps.reshape(degrees, wide), legendre.reshape(degrees, cycles), inv_noise.reshape(here, pixels),
    )
    return (most + rest).reshape(rows, 1, wide)


def solution(mesh):
    nband, nblk = mesh.shape["band"], mesh.shape["blk"]
    placed = (
        P(None, "blk", None),
        P("band", None),
        P("blk", None, None),
        P(),
        P(),
        P(),
        P("band", "blk", None),
    )
    return jax.shard_map(
        functools.partial(shards, nband, nblk),
        mesh=mesh, in_specs=placed, out_specs=P("band", "blk", None), check_vma=False,
    )
```

```python
import functools
import math

import jax
import jax.numpy as jnp
from jax import lax
from jax.experimental import pallas as pl
from jax.experimental.pallas import tpu as pltpu
from jax.sharding import PartitionSpec as P

MESH = pl.DeviceIdType.MESH
F32, BF16, I32 = jnp.float32, jnp.bfloat16, jnp.int32
LANES = 128
WIDE = 512
NY = 4
EARLY = 1


def dot_nt(a, b):
    return lax.dot_general(a, b, (((1,), (1,)), ((), ())), preferred_element_type=F32)


def split(x):
    high = x.astype(BF16)
    return high, (x - high.astype(F32)).astype(BF16)


def remainder(x, count, inverse):
    r = x - jnp.floor(x * inverse) * count
    r = jnp.where(r < 0.0, r + count, r)
    return jnp.where(r >= count, r - count, r)


def turn(doubled, count, inverse):
    k = jnp.floor(doubled * inverse + 0.5)
    phi = (doubled - k * count) * (inverse * jnp.float32(math.pi / 2))
    sq = phi * phi
    sin = phi + phi * sq * (-1.6666654611e-1 + sq * (8.3321608736e-3 + sq * -1.9515295891e-4))
    cos = 1.0 - 0.5 * sq + sq * sq * (
        4.166664568298827e-2 + sq * (-1.388731625493765e-3 + sq * 2.443315711809948e-5)
    )
    ki = k.astype(I32)
    odd = (ki & 1) == 1
    c = jnp.where(odd, sin, cos)
    s = jnp.where(odd, cos, sin)
    return jnp.where(((ki + 1) & 2) != 0, -c, c), jnp.where((ki & 2) != 0, s, -s)


def kernel(
    nband, nblk,
    m_in, order_in, counts_in, beam_in, amps_in, leg_in, noise_in,
    out_ref, rest_ref,
    m_ref, order_ref, counts_ref, beam_ref, amps_ref, leg_ref, noise_ref, in_sem,
    m_col, a_cos, a_sin, b_cos, b_sin, gram, flat, syn, got, stage, half, back, around, legp, beams, gains, inside,
    send_sem, recv_sem, own_sem, beam_sem, ag_send, ag_recv,
):
    band = lax.axis_index("band")
    me = lax.axis_index("blk")
    nz = nblk // NY
    nx = nband // 2
    degrees = leg_ref.shape[0]
    cycles = leg_ref.shape[1]
    orders = m_col.shape[0]
    here = cycles // nblk
    pixels = noise_ref.shape[1]
    steps = pixels // WIDE
    chains = amps_ref.shape[1] // 2
    rows = degrees // nband
    my_y, my_z = me // nz, me & (nz - 1)
    my_x, core = band // 2, band & 1

    column = [((my_y + k) & (NY - 1)) * nz for k in range(NY)]

    turns = (2, 1, 3, 0)

    def each_other(act, first, last):
        @pl.loop(first, min(last, nz - 1))
        def _(u):
            z = (my_z + nz // 2 + ((u >> 1) ^ -(u & 1))) & (nz - 1)
            for j, k in enumerate(turns):
                act(column[k] + z, u * NY + j)

        if last == nz:
            for j, k in enumerate(turns[:-1]):
                act(column[k] + my_z, (nz - 1) * NY + j)

    def band_of(dx, dc):
        return ((my_x + dx) & (nx - 1)) * 2 + ((core + dc) & 1)

    others = [(dx, dc) for dx in range(nx) for dc in range(2) if (dx, dc) != (0, 0)]

    barrier = pltpu.get_barrier_semaphore()

    loads = [
        pltpu.make_async_copy(source, target, in_sem.at[k])
        for k, (source, target) in enumerate(
            (
                (amps_in, amps_ref), (beam_in, beam_ref), (leg_in, leg_ref), (m_in, m_ref),
                (order_in, order_ref), (counts_in, counts_ref), (noise_in, noise_ref),
            )
        )
    ]
    each_other(lambda d, t: pl.semaphore_signal(barrier, inc=1, device_id=(band, d), device_id_type=MESH), 0, nz)

    for dx, dc in others:
        pl.semaphore_signal(barrier, inc=1, device_id=(band_of(dx, dc), me), device_id_type=MESH)

    for load in loads:
        load.start()

    for load in loads:
        load.wait()

    def synth_step(i, total):
        parts = []
        for h in range(2):
            at = pl.multiple_of(i * 2 * LANES + h * LANES, LANES)
            piece = amps_ref[pl.ds(at, LANES), :].astype(F32).T
            parts.append((piece * beam_ref[:, pl.ds(at, LANES)]).astype(BF16))
        weighted = jnp.concatenate(parts, axis=1)
        at = pl.multiple_of(i * 2 * LANES, LANES)
        return total + jnp.dot(weighted, leg_ref[pl.ds(at, 2 * LANES), :], preferred_element_type=F32)

    total = lax.fori_loop(0, degrees // (2 * LANES), synth_step, jnp.zeros((2 * chains, cycles), F32))
    flat[...] = total.T
    for i in range(here):
        syn[:, i, :] = flat[pl.ds(i, nblk, stride=here), :]

    @pl.loop(0, orders, unroll=8)
    def _(i):
        m_col[pl.ds(i, 1), :] = jnp.full((1, LANES), m_ref[i], I32).astype(F32)

    lane = lax.broadcasted_iota(I32, (1, LANES), 1)

    def cycle(i):
        q = order_ref[me * here + i]
        return counts_ref[q], q & 1

    m = m_col[...]
    count_v = jnp.full((1, LANES), 1, I32)
    parity_v = jnp.zeros((1, LANES), I32)
    pixel = lax.broadcasted_iota(I32, (1, pixels), 1)
    for i in range(here):
        n, parity = cycle(i)
        inside[i] = jnp.where(pixel < n, jnp.sqrt(noise_ref[i : i + 1, :]), 0.0)
        mine = lane // 16 == i
        count_v = jnp.where(mine, n, count_v)
        parity_v = jnp.where(mine, parity, parity_v)
    count_v = count_v.astype(F32)
    inverse_v = 1.0 / count_v
    entry = lane % 16
    coarse = entry < steps
    stride = jnp.where(coarse, entry * WIDE, (entry - steps) * LANES)
    parity_v = jnp.where(coarse, parity_v, 0)
    r = remainder(m * stride.astype(F32), count_v, inverse_v)
    ca, sa = turn(4.0 * r + 2.0 * m * parity_v.astype(F32), count_v, inverse_v)
    kinds = steps + WIDE // LANES
    for i in range(here):
        for e in range(kinds):
            t = i * 16 + e
            a_cos[i * kinds + e] = jnp.broadcast_to(ca[:, t : t + 1], (orders, LANES))
            a_sin[i * kinds + e] = jnp.broadcast_to(sa[:, t : t + 1], (orders, LANES))

    def form_gram(i):
        n, _ = cycle(i)
        count = jnp.full((1, LANES), n, I32).astype(F32)
        inverse = 1.0 / count
        r = remainder(m_col[...] * lane.astype(F32), count, inverse)
        c2, s2 = turn(4.0 * r, count, inverse)
        b_cos[:, :LANES], b_sin[:, :LANES] = c2, s2
        for g in range(1, WIDE // LANES):
            c1, s1 = a_cos[i * kinds + steps + g], a_sin[i * kinds + steps + g]
            b_cos[:, g * LANES : (g + 1) * LANES] = c1 * c2 - s1 * s2
            b_sin[:, g * LANES : (g + 1) * LANES] = s1 * c2 + c1 * s2

        def step(a, acc):
            c1, s1 = a_cos[i * kinds + a], a_sin[i * kinds + a]
            highs, lows = [], []
            for g in range(WIDE // LANES):
                c2, s2 = b_cos[:, g * LANES : (g + 1) * LANES], b_sin[:, g * LANES : (g + 1) * LANES]
                w = inside[i, :, pl.ds(pl.multiple_of(a * WIDE + g * LANES, LANES), LANES)]
                ch, cl = split((c1 * c2 - s1 * s2) * w)
                sh, sl = split((s1 * c2 + c1 * s2) * w)
                highs.append(jnp.concatenate([ch, sh], axis=0))
                lows.append(jnp.concatenate([cl, sl], axis=0))
            high, low = jnp.concatenate(highs, axis=1), jnp.concatenate(lows, axis=1)
            return acc + dot_nt(high, jnp.concatenate([high, low], axis=0))

        two = 2 * orders
        acc = lax.fori_loop(0, steps, step, jnp.zeros((two, 2 * two), F32))
        cross = acc[:, two:]
        full = acc[:, :two] + (cross + cross.T)
        full = full * inverse[:, :two] if two <= LANES else full * inverse[:, :1]
        full = jnp.concatenate([full[:orders], pltpu.roll(full[orders:], orders, 1)], axis=0)
        gram[i] = jnp.concatenate(split(full), axis=0)

    @pl.loop(0, EARLY)
    def _(i):
        form_gram(i)

    pl.semaphore_wait(barrier, nblk - 1 + nband - 1)

    def send(d, t):
        pltpu.make_async_remote_copy(
            src_ref=syn.at[d], dst_ref=got.at[me], send_sem=send_sem.at[0], recv_sem=recv_sem.at[0],
            device_id=(band, d), device_id_type=MESH,
        ).start()

    each_other(send, 0, nz)
    pltpu.make_async_copy(syn.at[me], got.at[me], own_sem.at[0]).start()
    for dx, dc in others:
        pltpu.make_async_remote_copy(
            src_ref=beam_ref, dst_ref=beams.at[band], send_sem=beam_sem.at[0], recv_sem=beam_sem.at[1],
            device_id=(band_of(dx, dc), me), device_id_type=MESH,
        ).start()
    pltpu.make_async_copy(beam_ref, beams.at[band], own_sem.at[1]).start()

    @pl.loop(EARLY, here)
    def _(i):
        form_gram(i)

    row = lax.broadcasted_iota(I32, (cycles, cycles), 0)
    col = lax.broadcasted_iota(I32, (cycles, cycles), 1)
    slot = col % (nblk // 2) + col // (cycles // 2) * (nblk // 2)
    u, j = slot // NY, slot % NY
    k = jnp.where(j == 3, 0, jnp.where(j == 2, 3, 2 - j))
    z = (my_z - nz // 2 - ((u >> 1) ^ -(u & 1))) & (nz - 1)
    source = ((my_y - k) & (NY - 1)) * nz + z
    pick = jnp.where(row == here * source + col // (nblk // 2) % here, 1.0, 0.0).astype(BF16)
    mine = leg_ref[pl.ds(pl.multiple_of(band * rows, rows & -rows), rows), :]
    legp[...] = jnp.dot(mine, pick, preferred_element_type=F32).astype(BF16)

    pltpu.make_async_copy(syn.at[me], got.at[me], own_sem.at[0]).wait()
    most = got.at[pl.ds(0, nblk - 1)]
    pltpu.make_async_copy(most, most, recv_sem.at[0]).wait()

    for i in range(here):
        x = got[:, i, :]
        xh, xl = split(jnp.concatenate([x, pltpu.roll(x, chains, 1)], axis=0))
        y = jnp.dot(gram[i], jnp.concatenate([xh, xl], axis=1), preferred_element_type=F32)
        wide, two = 2 * chains, 2 * orders
        y = (y[:two, :wide] + y[:two, wide:]) + (y[two:, :wide] + y[two:, wide:])
        lane_k = lax.broadcasted_iota(I32, (orders, wide), 1)
        stage[:, i, :] = jnp.where(lane_k < chains, y[:orders], y[orders:])
    half[...] = stage[...].astype(BF16)

    for g in range(2):

        def send(d, t, g=g):
            pltpu.make_async_remote_copy(
                src_ref=half.at[d], dst_ref=back.at[t], send_sem=send_sem.at[1], recv_sem=recv_sem.at[1 + g],
                device_id=(band, d), device_id_type=MESH,
            ).start()

        each_other(send, g * nz // 2, (g + 1) * nz // 2)

    pltpu.make_async_copy(half.at[me], back.at[nblk - 1], own_sem.at[2]).start()

    pltpu.make_async_copy(beam_ref, beams.at[band], own_sem.at[1]).wait()
    pltpu.make_async_copy(beams.at[pl.ds(0, nband - 1)], beams.at[pl.ds(0, nband - 1)], beam_sem.at[1]).wait()
    first = band * rows
    base = first // LANES * LANES
    span = -(-(rows + LANES // 2) // LANES) * LANES
    for b in range(nband):
        line = beams[b, :, pl.ds(pl.multiple_of(base, LANES), span)]
        if rows % LANES:
            line = jnp.where(first - base > 0, pltpu.roll(line, span - LANES // 2, 1), line)
        for g in range(-(-rows // LANES)):
            size = min(LANES, rows - g * LANES)
            block = jnp.broadcast_to(line[:, g * LANES : (g + 1) * LANES], (LANES, LANES)).T
            gains[b, g * LANES : g * LANES + size, :] = block[:size]

    per = cycles // 2

    def across(dx, dc, g):
        part = around.at[band, pl.ds(g * per, per)]
        k = (g * nx + dx) * 2 + dc
        return pltpu.make_async_remote_copy(
            src_ref=part, dst_ref=part, send_sem=ag_send.at[k], recv_sem=ag_recv.at[k],
            device_id=(band_of(dx, dc), me), device_id_type=MESH,
        )

    def arrived(dx, dc, g):
        part = around.at[band_of(-dx, dc), pl.ds(g * per, per)]
        pltpu.make_async_copy(part, part, ag_recv.at[(g * nx + dx) * 2 + dc]).wait()

    far = nx // 2
    near = [dx for dx in range(1, nx) if dx != far]
    direct = [(far, 0), (far, 1), (0, 1)] + [(dx, dc) for dc in range(2) for dx in near]
    for g in (1, 0):
        lot = nblk // 2
        if g == 1:
            pltpu.make_async_copy(half.at[me], back.at[nblk - 1], own_sem.at[2]).wait()
        most = back.at[pl.ds(g * lot, lot - g)]
        pltpu.make_async_copy(most, most, recv_sem.at[1 + g]).wait()
        stage[g * lot : (g + 1) * lot] = back[g * lot : (g + 1) * lot].astype(F32)
        for i in range(here):
            at = g * per + i * lot
            around[band, at : at + lot, :] = stage[g * lot : (g + 1) * lot, i, :].astype(BF16)
        for dx, dc in direct:
            across(dx, dc, g).start()

    def terms(slots):
        total = None
        for i in range(0, len(slots), 2):
            pair = slots[i : i + 2]
            side = jnp.concatenate([around[slot] for slot in pair], axis=1) if len(pair) == 2 else around[pair[0]]
            both = jnp.dot(legp[...], side, preferred_element_type=F32)
            wide = 2 * chains
            for j, slot in enumerate(pair):
                one = gains[slot] * both[:, j * wide : (j + 1) * wide]
                total = one if total is None else total + one
        return total

    for g in (1, 0):
        arrived(0, 1, g)
        arrived(far, 0, g)
        for dx in near:
            arrived(dx, 0, g)
    out_ref[...] = terms([band, band_of(0, 1), band_of(-far, 0)] + [band_of(-dx, 0) for dx in near[:1]])
    for g in (1, 0):
        for dx in near:
            arrived(dx, 1, g)
        arrived(far, 1, g)
    rest_ref[...] = terms([band_of(-dx, 0) for dx in near[1:]] + [band_of(-dx, 1) for dx in near] + [band_of(-far, 1)])

    for g in (1, 0):
        for dx, dc in direct:
            across(dx, dc, g).wait_send()
    for k in range(nband - 1):
        pltpu.make_async_copy(beam_ref, beam_ref, beam_sem.at[0]).wait()
    most = syn.at[pl.ds(0, nblk - 1)]
    pltpu.make_async_copy(most, most, send_sem.at[0]).wait()
    most = half.at[pl.ds(0, nblk - 1)]
    pltpu.make_async_copy(most, most, send_sem.at[1]).wait()


def shards(nband, nblk, amps, beam, legendre, m_values, cycle_order, pixel_counts, inv_noise):
    degrees, _, wide = amps.shape
    cycles = legendre.shape[2]
    orders = m_values.shape[0]
    here = cycles // nblk
    pixels = inv_noise.shape[2]
    rows = degrees // nband
    steps = pixels // WIDE
    vmem = pl.BlockSpec(memory_space=pltpu.VMEM)
    left = pl.BlockSpec(memory_space=pl.ANY)
    dma = pltpu.SemaphoreType.DMA
    most, rest = pl.pallas_call(
        functools.partial(kernel, nband, nblk),
        out_shape=[pltpu.VMEM((rows, wide), F32)] * 2,
        in_specs=[left] * 7,
        out_specs=[vmem, vmem],
        scratch_shapes=[
            pltpu.SMEM((orders,), I32),
            pltpu.SMEM((cycles,), I32),
            pltpu.SMEM((cycles,), I32),
            pltpu.VMEM((1, degrees), F32),
            pltpu.VMEM((degrees, wide), BF16),
            pltpu.VMEM((degrees, cycles), BF16),
            pltpu.VMEM((here, pixels), F32),
            dma((7,)),
            pltpu.VMEM((orders, LANES), F32),
            pltpu.VMEM((here * (steps + WIDE // LANES), orders, LANES), F32),
            pltpu.VMEM((here * (steps + WIDE // LANES), orders, LANES), F32),
            pltpu.VMEM((orders, WIDE), F32),
            pltpu.VMEM((orders, WIDE), F32),
            pltpu.VMEM((here, 4 * orders, 2 * orders), BF16),
            pltpu.VMEM((cycles, wide), F32),
            pltpu.VMEM((nblk, here, wide), F32),
            pltpu.VMEM((nblk, here, wide), F32),
            pltpu.VMEM((orders, here, wide), F32),
            pltpu.VMEM((orders, here, wide), BF16),
            pltpu.VMEM((nblk, here, wide), BF16),
            pltpu.VMEM((nband, cycles, wide), BF16),
            pltpu.VMEM((rows, cycles), BF16),
            pltpu.VMEM((nband, 1, degrees), F32),
            pltpu.VMEM((nband, rows, wide), F32),
            pltpu.VMEM((here, 1, pixels), F32),
            dma((2,)),
            dma((3,)),
            dma((3,)),
            dma((2,)),
            dma((2 * nband,)),
            dma((2 * nband,)),
        ],
        compiler_params=pltpu.CompilerParams(
            collective_id=0, has_side_effects=True, vmem_limit_bytes=60 * 1024 * 1024
        ),
    )(
        m_values, cycle_order, pixel_counts,
        beam, amps.reshape(degrees, wide), legendre.reshape(degrees, cycles), inv_noise.reshape(here, pixels),
    )
    return (most + rest).reshape(rows, 1, wide)


def solution(mesh):
    nband, nblk = mesh.shape["band"], mesh.shape["blk"]
    placed = (
        P(None, "blk", None),
        P("band", None),
        P("blk", None, None),
        P(),
        P(),
        P(),
        P("band", "blk", None),
    )
    return jax.shard_map(
        functools.partial(shards, nband, nblk),
        mesh=mesh, in_specs=placed, out_specs=P("band", "blk", None), check_vma=False,
    )
```

```python
import functools
import math

import jax
import jax.numpy as jnp
from jax import lax
from jax.experimental import pallas as pl
from jax.experimental.pallas import tpu as pltpu
from jax.sharding import PartitionSpec as P

MESH = pl.DeviceIdType.MESH
F32, BF16, I32 = jnp.float32, jnp.bfloat16, jnp.int32
LANES = 128
WIDE = 512
NY = 4
EARLY = 0


def dot_nt(a, b):
    return lax.dot_general(a, b, (((1,), (1,)), ((), ())), preferred_element_type=F32)


def split(x):
    high = x.astype(BF16)
    return high, (x - high.astype(F32)).astype(BF16)


def remainder(x, count, inverse):
    r = x - jnp.floor(x * inverse) * count
    r = jnp.where(r < 0.0, r + count, r)
    return jnp.where(r >= count, r - count, r)


def turn(doubled, count, inverse):
    k = jnp.floor(doubled * inverse + 0.5)
    phi = (doubled - k * count) * (inverse * jnp.float32(math.pi / 2))
    sq = phi * phi
    sin = phi + phi * sq * (-1.6666654611e-1 + sq * (8.3321608736e-3 + sq * -1.9515295891e-4))
    cos = 1.0 - 0.5 * sq + sq * sq * (
        4.166664568298827e-2 + sq * (-1.388731625493765e-3 + sq * 2.443315711809948e-5)
    )
    ki = k.astype(I32)
    odd = (ki & 1) == 1
    c = jnp.where(odd, sin, cos)
    s = jnp.where(odd, cos, sin)
    return jnp.where(((ki + 1) & 2) != 0, -c, c), jnp.where((ki & 2) != 0, s, -s)


def kernel(
    nband, nblk,
    m_in, order_in, counts_in, beam_in, amps_in, leg_in, noise_in,
    out_ref, rest_ref,
    m_ref, order_ref, counts_ref, beam_ref, amps_ref, leg_ref, noise_ref, in_sem,
    m_col, a_cos, a_sin, b_cos, b_sin, gram, flat, syn, got, stage, half, back, around, legp, beams, gains, inside,
    send_sem, recv_sem, own_sem, beam_sem, ag_send, ag_recv,
):
    band = lax.axis_index("band")
    me = lax.axis_index("blk")
    nz = nblk // NY
    nx = nband // 2
    degrees = leg_ref.shape[0]
    cycles = leg_ref.shape[1]
    orders = m_col.shape[0]
    here = cycles // nblk
    pixels = noise_ref.shape[1]
    steps = pixels // WIDE
    chains = amps_ref.shape[1] // 2
    rows = degrees // nband
    my_y, my_z = me // nz, me & (nz - 1)
    my_x, core = band // 2, band & 1

    column = [((my_y + k) & (NY - 1)) * nz for k in range(NY)]

    turns = (2, 1, 3, 0)

    def each_other(act, first, last):
        @pl.loop(first, min(last, nz - 1))
        def _(u):
            z = (my_z + nz // 2 + ((u >> 1) ^ -(u & 1))) & (nz - 1)
            for j, k in enumerate(turns):
                act(column[k] + z, u * NY + j)

        if last == nz:
            for j, k in enumerate(turns[:-1]):
                act(column[k] + my_z, (nz - 1) * NY + j)

    def band_of(dx, dc):
        return ((my_x + dx) & (nx - 1)) * 2 + ((core + dc) & 1)

    others = [(dx, dc) for dx in range(nx) for dc in range(2) if (dx, dc) != (0, 0)]

    barrier = pltpu.get_barrier_semaphore()

    loads = [
        pltpu.make_async_copy(source, target, in_sem.at[k])
        for k, (source, target) in enumerate(
            (
                (amps_in, amps_ref), (beam_in, beam_ref), (leg_in, leg_ref), (m_in, m_ref),
                (order_in, order_ref), (counts_in, counts_ref), (noise_in, noise_ref),
            )
        )
    ]
    each_other(lambda d, t: pl.semaphore_signal(barrier, inc=1, device_id=(band, d), device_id_type=MESH), 0, nz)

    for dx, dc in others:
        pl.semaphore_signal(barrier, inc=1, device_id=(band_of(dx, dc), me), device_id_type=MESH)

    for load in loads:
        load.start()

    for load in loads:
        load.wait()

    def synth_step(i, total):
        parts = []
        for h in range(2):
            at = pl.multiple_of(i * 2 * LANES + h * LANES, LANES)
            piece = amps_ref[pl.ds(at, LANES), :].astype(F32).T
            parts.append((piece * beam_ref[:, pl.ds(at, LANES)]).astype(BF16))
        weighted = jnp.concatenate(parts, axis=1)
        at = pl.multiple_of(i * 2 * LANES, LANES)
        return total + jnp.dot(weighted, leg_ref[pl.ds(at, 2 * LANES), :], preferred_element_type=F32)

    total = lax.fori_loop(0, degrees // (2 * LANES), synth_step, jnp.zeros((2 * chains, cycles), F32))
    flat[...] = total.T
    for i in range(here):
        syn[:, i, :] = flat[pl.ds(i, nblk, stride=here), :]

    @pl.loop(0, orders, unroll=8)
    def _(i):
        m_col[pl.ds(i, 1), :] = jnp.full((1, LANES), m_ref[i], I32).astype(F32)

    lane = lax.broadcasted_iota(I32, (1, LANES), 1)

    def cycle(i):
        q = order_ref[me * here + i]
        return counts_ref[q], q & 1

    m = m_col[...]
    count_v = jnp.full((1, LANES), 1, I32)
    parity_v = jnp.zeros((1, LANES), I32)
    pixel = lax.broadcasted_iota(I32, (1, pixels), 1)
    for i in range(here):
        n, parity = cycle(i)
        inside[i] = jnp.where(pixel < n, jnp.sqrt(noise_ref[i : i + 1, :]), 0.0)
        mine = lane // 16 == i
        count_v = jnp.where(mine, n, count_v)
        parity_v = jnp.where(mine, parity, parity_v)
    count_v = count_v.astype(F32)
    inverse_v = 1.0 / count_v
    entry = lane % 16
    coarse = entry < steps
    stride = jnp.where(coarse, entry * WIDE, (entry - steps) * LANES)
    parity_v = jnp.where(coarse, parity_v, 0)
    r = remainder(m * stride.astype(F32), count_v, inverse_v)
    ca, sa = turn(4.0 * r + 2.0 * m * parity_v.astype(F32), count_v, inverse_v)
    kinds = steps + WIDE // LANES
    for i in range(here):
        for e in range(kinds):
            t = i * 16 + e
            a_cos[i * kinds + e] = jnp.broadcast_to(ca[:, t : t + 1], (orders, LANES))
            a_sin[i * kinds + e] = jnp.broadcast_to(sa[:, t : t + 1], (orders, LANES))

    def form_gram(i):
        n, _ = cycle(i)
        count = jnp.full((1, LANES), n, I32).astype(F32)
        inverse = 1.0 / count
        r = remainder(m_col[...] * lane.astype(F32), count, inverse)
        c2, s2 = turn(4.0 * r, count, inverse)
        b_cos[:, :LANES], b_sin[:, :LANES] = c2, s2
        for g in range(1, WIDE // LANES):
            c1, s1 = a_cos[i * kinds + steps + g], a_sin[i * kinds + steps + g]
            b_cos[:, g * LANES : (g + 1) * LANES] = c1 * c2 - s1 * s2
            b_sin[:, g * LANES : (g + 1) * LANES] = s1 * c2 + c1 * s2

        def step(a, acc):
            c1, s1 = a_cos[i * kinds + a], a_sin[i * kinds + a]
            highs, lows = [], []
            for g in range(WIDE // LANES):
                c2, s2 = b_cos[:, g * LANES : (g + 1) * LANES], b_sin[:, g * LANES : (g + 1) * LANES]
                w = inside[i, :, pl.ds(pl.multiple_of(a * WIDE + g * LANES, LANES), LANES)]
                ch, cl = split((c1 * c2 - s1 * s2) * w)
                sh, sl = split((s1 * c2 + c1 * s2) * w)
                highs.append(jnp.concatenate([ch, sh], axis=0))
                lows.append(jnp.concatenate([cl, sl], axis=0))
            high, low = jnp.concatenate(highs, axis=1), jnp.concatenate(lows, axis=1)
            return acc + dot_nt(high, jnp.concatenate([high, low], axis=0))

        two = 2 * orders
        acc = lax.fori_loop(0, steps, step, jnp.zeros((two, 2 * two), F32))
        cross = acc[:, two:]
        full = acc[:, :two] + (cross + cross.T)
        full = full * inverse[:, :two] if two <= LANES else full * inverse[:, :1]
        full = jnp.concatenate([full[:orders], pltpu.roll(full[orders:], orders, 1)], axis=0)
        gram[i] = jnp.concatenate(split(full), axis=0)

    @pl.loop(0, EARLY)
    def _(i):
        form_gram(i)

    pl.semaphore_wait(barrier, nblk - 1 + nband - 1)

    def send(d, t):
        pltpu.make_async_remote_copy(
            src_ref=syn.at[d], dst_ref=got.at[me], send_sem=send_sem.at[0], recv_sem=recv_sem.at[0],
            device_id=(band, d), device_id_type=MESH,
        ).start()

    each_other(send, 0, nz)
    pltpu.make_async_copy(syn.at[me], got.at[me], own_sem.at[0]).start()
    for dx, dc in others:
        pltpu.make_async_remote_copy(
            src_ref=beam_ref, dst_ref=beams.at[band], send_sem=beam_sem.at[0], recv_sem=beam_sem.at[1],
            device_id=(band_of(dx, dc), me), device_id_type=MESH,
        ).start()
    pltpu.make_async_copy(beam_ref, beams.at[band], own_sem.at[1]).start()

    @pl.loop(EARLY, here)
    def _(i):
        form_gram(i)

    pltpu.make_async_copy(syn.at[me], got.at[me], own_sem.at[0]).wait()
    most = got.at[pl.ds(0, nblk - 1)]
    pltpu.make_async_copy(most, most, recv_sem.at[0]).wait()

    for i in range(here):
        x = got[:, i, :]
        xh, xl = split(jnp.concatenate([x, pltpu.roll(x, chains, 1)], axis=0))
        y = jnp.dot(gram[i], jnp.concatenate([xh, xl], axis=1), preferred_element_type=F32)
        wide, two = 2 * chains, 2 * orders
        y = (y[:two, :wide] + y[:two, wide:]) + (y[two:, :wide] + y[two:, wide:])
        lane_k = lax.broadcasted_iota(I32, (orders, wide), 1)
        stage[:, i, :] = jnp.where(lane_k < chains, y[:orders], y[orders:])
    half[...] = stage[...].astype(BF16)

    for g in range(2):

        def send(d, t, g=g):
            pltpu.make_async_remote_copy(
                src_ref=half.at[d], dst_ref=back.at[t], send_sem=send_sem.at[1], recv_sem=recv_sem.at[1 + g],
                device_id=(band, d), device_id_type=MESH,
            ).start()

        each_other(send, g * nz // 2, (g + 1) * nz // 2)

    pltpu.make_async_copy(half.at[me], back.at[nblk - 1], own_sem.at[2]).start()

    row = lax.broadcasted_iota(I32, (cycles, cycles), 0)
    col = lax.broadcasted_iota(I32, (cycles, cycles), 1)
    slot = col % (nblk // 2) + col // (cycles // 2) * (nblk // 2)
    u, j = slot // NY, slot % NY
    k = jnp.where(j == 3, 0, jnp.where(j == 2, 3, 2 - j))
    z = (my_z - nz // 2 - ((u >> 1) ^ -(u & 1))) & (nz - 1)
    source = ((my_y - k) & (NY - 1)) * nz + z
    pick = jnp.where(row == here * source + col // (nblk // 2) % here, 1.0, 0.0).astype(BF16)
    mine = leg_ref[pl.ds(pl.multiple_of(band * rows, rows & -rows), rows), :]
    legp[...] = jnp.dot(mine, pick, preferred_element_type=F32).astype(BF16)

    pltpu.make_async_copy(beam_ref, beams.at[band], own_sem.at[1]).wait()
    pltpu.make_async_copy(beams.at[pl.ds(0, nband - 1)], beams.at[pl.ds(0, nband - 1)], beam_sem.at[1]).wait()
    first = band * rows
    base = first // LANES * LANES
    span = -(-(rows + LANES // 2) // LANES) * LANES
    for b in range(nband):
        line = beams[b, :, pl.ds(pl.multiple_of(base, LANES), span)]
        if rows % LANES:
            line = jnp.where(first - base > 0, pltpu.roll(line, span - LANES // 2, 1), line)
        for g in range(-(-rows // LANES)):
            size = min(LANES, rows - g * LANES)
            block = jnp.broadcast_to(line[:, g * LANES : (g + 1) * LANES], (LANES, LANES)).T
            gains[b, g * LANES : g * LANES + size, :] = block[:size]

    per = cycles // 2

    def across(dx, dc, g):
        part = around.at[band, pl.ds(g * per, per)]
        k = (g * nx + dx) * 2 + dc
        return pltpu.make_async_remote_copy(
            src_ref=part, dst_ref=part, send_sem=ag_send.at[k], recv_sem=ag_recv.at[k],
            device_id=(band_of(dx, dc), me), device_id_type=MESH,
        )

    def arrived(dx, dc, g):
        part = around.at[band_of(-dx, dc), pl.ds(g * per, per)]
        pltpu.make_async_copy(part, part, ag_recv.at[(g * nx + dx) * 2 + dc]).wait()

    far = nx // 2
    near = [dx for dx in range(1, nx) if dx != far]
    direct = [(far, 0), (far, 1), (0, 1)] + [(dx, dc) for dc in range(2) for dx in near]
    for g in (1, 0):
        lot = nblk // 2
        if g == 1:
            pltpu.make_async_copy(half.at[me], back.at[nblk - 1], own_sem.at[2]).wait()
        most = back.at[pl.ds(g * lot, lot - g)]
        pltpu.make_async_copy(most, most, recv_sem.at[1 + g]).wait()
        stage[g * lot : (g + 1) * lot] = back[g * lot : (g + 1) * lot].astype(F32)
        for i in range(here):
            at = g * per + i * lot
            around[band, at : at + lot, :] = stage[g * lot : (g + 1) * lot, i, :].astype(BF16)
        for dx, dc in direct:
            across(dx, dc, g).start()

    def terms(slots):
        total = None
        for i in range(0, len(slots), 2):
            pair = slots[i : i + 2]
            side = jnp.concatenate([around[slot] for slot in pair], axis=1) if len(pair) == 2 else around[pair[0]]
            both = jnp.dot(legp[...], side, preferred_element_type=F32)
            wide = 2 * chains
            for j, slot in enumerate(pair):
                one = gains[slot] * both[:, j * wide : (j + 1) * wide]
                total = one if total is None else total + one
        return total

    for g in (1, 0):
        arrived(0, 1, g)
        arrived(far, 0, g)
        for dx in near:
            arrived(dx, 0, g)
    out_ref[...] = terms([band, band_of(0, 1), band_of(-far, 0)] + [band_of(-dx, 0) for dx in near[:1]])
    for g in (1, 0):
        for dx in near:
            arrived(dx, 1, g)
        arrived(far, 1, g)
    rest_ref[...] = terms([band_of(-dx, 0) for dx in near[1:]] + [band_of(-dx, 1) for dx in near] + [band_of(-far, 1)])

    for g in (1, 0):
        for dx, dc in direct:
            across(dx, dc, g).wait_send()
    for k in range(nband - 1):
        pltpu.make_async_copy(beam_ref, beam_ref, beam_sem.at[0]).wait()
    most = syn.at[pl.ds(0, nblk - 1)]
    pltpu.make_async_copy(most, most, send_sem.at[0]).wait()
    most = half.at[pl.ds(0, nblk - 1)]
    pltpu.make_async_copy(most, most, send_sem.at[1]).wait()


def shards(nband, nblk, amps, beam, legendre, m_values, cycle_order, pixel_counts, inv_noise):
    degrees, _, wide = amps.shape
    cycles = legendre.shape[2]
    orders = m_values.shape[0]
    here = cycles // nblk
    pixels = inv_noise.shape[2]
    rows = degrees // nband
    steps = pixels // WIDE
    vmem = pl.BlockSpec(memory_space=pltpu.VMEM)
    left = pl.BlockSpec(memory_space=pl.ANY)
    dma = pltpu.SemaphoreType.DMA
    most, rest = pl.pallas_call(
        functools.partial(kernel, nband, nblk),
        out_shape=[pltpu.VMEM((rows, wide), F32)] * 2,
        in_specs=[left] * 7,
        out_specs=[vmem, vmem],
        scratch_shapes=[
            pltpu.SMEM((orders,), I32),
            pltpu.SMEM((cycles,), I32),
            pltpu.SMEM((cycles,), I32),
            pltpu.VMEM((1, degrees), F32),
            pltpu.VMEM((degrees, wide), BF16),
            pltpu.VMEM((degrees, cycles), BF16),
            pltpu.VMEM((here, pixels), F32),
            dma((7,)),
            pltpu.VMEM((orders, LANES), F32),
            pltpu.VMEM((here * (steps + WIDE // LANES), orders, LANES), F32),
            pltpu.VMEM((here * (steps + WIDE // LANES), orders, LANES), F32),
            pltpu.VMEM((orders, WIDE), F32),
            pltpu.VMEM((orders, WIDE), F32),
            pltpu.VMEM((here, 4 * orders, 2 * orders), BF16),
            pltpu.VMEM((cycles, wide), F32),
            pltpu.VMEM((nblk, here, wide), F32),
            pltpu.VMEM((nblk, here, wide), F32),
            pltpu.VMEM((orders, here, wide), F32),
            pltpu.VMEM((orders, here, wide), BF16),
            pltpu.VMEM((nblk, here, wide), BF16),
            pltpu.VMEM((nband, cycles, wide), BF16),
            pltpu.VMEM((rows, cycles), BF16),
            pltpu.VMEM((nband, 1, degrees), F32),
            pltpu.VMEM((nband, rows, wide), F32),
            pltpu.VMEM((here, 1, pixels), F32),
            dma((2,)),
            dma((3,)),
            dma((3,)),
            dma((2,)),
            dma((2 * nband,)),
            dma((2 * nband,)),
        ],
        compiler_params=pltpu.CompilerParams(
            collective_id=0, has_side_effects=True, vmem_limit_bytes=60 * 1024 * 1024
        ),
    )(
        m_values, cycle_order, pixel_counts,
        beam, amps.reshape(degrees, wide), legendre.reshape(degrees, cycles), inv_noise.reshape(here, pixels),
    )
    return (most + rest).reshape(rows, 1, wide)


def solution(mesh):
    nband, nblk = mesh.shape["band"], mesh.shape["blk"]
    placed = (
        P(None, "blk", None),
        P("band", None),
        P("blk", None, None),
        P(),
        P(),
        P(),
        P("band", "blk", None),
    )
    return jax.shard_map(
        functools.partial(shards, nband, nblk),
        mesh=mesh, in_specs=placed, out_specs=P("band", "blk", None), check_vma=False,
    )
```
